512 devices in a mesh: shot: 16 (over x, y_hi), dom: 32 (over y_lo, z, core).
Axes of the slice: x: 4, y: 8 (y_hi: 4, y_lo: 2; y = y_hi * 2 + y_lo), z: 8, core: 2. Of those that a mesh axis runs over, the one named last changes fastest.
Arguments:
- velocity: float32 [512, 8, 8, 128], P(('shot', 'dom')), may hold values from 1.5 to 4.5
- aperture: int32 [16, 32, 2], P('shot', 'dom'), may hold values from 0 to 511, as said below
- source_cell: int32 [16], P('shot'), may hold values from 0 to 524287
- wavelet: float32 [16, 64], P('shot'), may hold values from -6 to 6
- observed: float32 [16, 64, 256], P('shot'), may hold values from -6 to 6
- receivers: int32 [16, 256], P('shot'), may hold values from 0 to 524287
- checkpoint: int32 [16], P('shot'), may hold values from 0 to 56
- forward_previous: float32 [16, 256, 16, 128], P('shot', 'dom'), may hold values from -6 to 6
- forward_current: float32 [16, 256, 16, 128], P('shot', 'dom'), may hold values from -6 to 6
- adjoint_next: float32 [16, 256, 16, 128], P('shot', 'dom'), may hold values from -6 to 6
- adjoint_current: float32 [16, 256, 16, 128], P('shot', 'dom'), may hold values from -6 to 6
Outputs:
- gradient: float32 [512, 8, 8, 128], P(('shot', 'dom'))
The draws below stay inside these ranges and needn't reach their ends.
Inputs may be any that keep to these rules, and one draw needn't show every extreme that they name: For each group g there is a start row s_g with aperture[g, d, k] = (s_g + k) * 32 + d: the group's aperture is 2 consecutive rows of tiles across all slabs. Start rows repeat among groups.
All inputs are finite; a program needn't handle non-finite values.
Results may differ from the reference program's by a relative error of at most 0.0003.
Values sent between devices are 32-bit elements; how exact they have to be, the bound alone decides.
No kernel may reach another device: no remote copies, remote signals or barrier semaphores. Data moves between devices by JAX's collectives and lax.ppermute only.
A program may use at most 64 MiB of HBM per device.

```python
import jax
import jax.numpy as jnp
from jax import lax

TX = 8
TY = 8
TZ = 128
APER = 2
STEPS = 8
NT = 64
NREC = 256
GROUPS = 16
SLABS = 32
TILES = 512
NXA = 256
AY = 16


def draw_aperture(key, part):
    first_key, second_key = jax.random.split(key)
    starts = jax.random.randint(first_key, (GROUPS,), 0, GROUPS - APER + 1).astype(jnp.int32)
    chosen = jax.random.permutation(second_key, GROUPS)
    starts = starts.at[chosen[0]].set(GROUPS - APER)
    starts = starts.at[chosen[1]].set(0)
    slab_ids = jnp.arange(SLABS, dtype=jnp.int32)
    layers = jnp.arange(APER, dtype=jnp.int32)
    return ((starts[:, None, None] + layers[None, None, :]) * SLABS + slab_ids[None, :, None]).astype(jnp.int32)


def place_ends(drawn, own_key, least, high):
    dims = drawn.shape
    place = [jax.random.randint(jax.random.fold_in(own_key, axis), (), 0, dims[axis]) for axis in range(len(dims))]
    drawn = drawn.at[tuple(place)].set(least)
    longest = dims.index(max(dims))
    place[longest] = (place[longest] + 1) % dims[longest]
    return drawn.at[tuple(place)].set(high)


def block_levels(own_key, shape, cuts, least, high):
    level = 1.0
    for axis_at, shards_of in cuts:
        draws = jax.random.uniform(jax.random.fold_in(jax.random.fold_in(own_key, 6), axis_at), (shards_of,), jnp.float32, least / len(cuts), high / len(cuts))
        level = level * jnp.repeat(jnp.exp(draws), shape[axis_at] // shards_of).reshape((-1,) + (1,) * (len(shape) - 1 - axis_at))
    return level


def noise(stream_key, shape, spread, bound, cuts=(), kind=jnp.bfloat16):
    entries = jax.random.normal(stream_key, shape, jnp.float32) * spread
    if len(cuts) > 0:
        entries = block_levels(stream_key, shape, cuts, -0.22, 0.18) * entries
    return jnp.clip(entries, min=-bound, max=bound).astype(kind)


def setup_inputs(seed: int = 0) -> dict:
    key_list = jax.random.split(jax.random.key(seed), 12)
    velocity = jnp.clip(1.5 + 3.0 * jax.random.uniform(key_list[0], (TILES, TX, TY, TZ), jnp.float32) ** block_levels(key_list[0], (TILES, TX, TY, TZ), ((0, 512),), -0.2, 0.2), 1.5, 4.5)
    aperture = draw_aperture(jax.random.fold_in(key_list[11], 71), 0)
    source_cell = place_ends(jax.random.randint(key_list[2], (GROUPS,), 0, NXA * AY * TZ), jax.random.fold_in(key_list[2], 1), 0, (NXA * AY * TZ) - 1).astype(jnp.int32)
    wavelet = noise(key_list[3], (GROUPS, NT), 1.0, 6.0, ((0, 16),), jnp.float32)
    observed = noise(key_list[4], (GROUPS, NT, NREC), 1.0, 6.0, ((0, 16),), jnp.float32)
    receivers = place_ends(jax.random.randint(key_list[5], (GROUPS, NREC), 0, NXA * AY * TZ), jax.random.fold_in(key_list[5], 1), 0, (NXA * AY * TZ) - 1).astype(jnp.int32)
    checkpoint = place_ends(jax.random.randint(key_list[6], (GROUPS,), 0, NT - STEPS + 1), jax.random.fold_in(key_list[6], 1), 0, NT - STEPS).astype(jnp.int32)
    forward_previous = noise(key_list[7], (GROUPS, NXA, AY, TZ), 1.0, 6.0, ((0, 16), (1, 32)), jnp.float32)
    forward_current = noise(key_list[8], (GROUPS, NXA, AY, TZ), 1.0, 6.0, ((0, 16), (1, 32)), jnp.float32)
    adjoint_next = noise(key_list[9], (GROUPS, NXA, AY, TZ), 1.0, 6.0, ((0, 16), (1, 32)), jnp.float32)
    adjoint_current = noise(key_list[10], (GROUPS, NXA, AY, TZ), 1.0, 6.0, ((0, 16), (1, 32)), jnp.float32)
    return dict(velocity=velocity, aperture=aperture, source_cell=source_cell, wavelet=wavelet, observed=observed, receivers=receivers, checkpoint=checkpoint, forward_previous=forward_previous, forward_current=forward_current, adjoint_next=adjoint_next, adjoint_current=adjoint_current)


STENCIL_WEIGHTS = (-205.0 / 72.0, 8.0 / 5.0, -1.0 / 5.0, 8.0 / 315.0, -1.0 / 560.0)
STEP_SCALE = 0.088


def laplace(field, padded_x):
    extent_x, extent_y, extent_z = field.shape
    padded = jnp.pad(padded_x, ((0, 0), (4, 4), (4, 4)))
    middle = padded[4:4 + extent_x, 4:4 + extent_y, 4:4 + extent_z]
    accumulated = (3.0 * STENCIL_WEIGHTS[0]) * middle
    for offset in range(1, 5):
        neighbours = padded[4 + offset:4 + offset + extent_x, 4:4 + extent_y, 4:4 + extent_z] + padded[4 - offset:4 - offset + extent_x, 4:4 + extent_y, 4:4 + extent_z]
        neighbours = neighbours + padded[4:4 + extent_x, 4 + offset:4 + offset + extent_y, 4:4 + extent_z] + padded[4:4 + extent_x, 4 - offset:4 - offset + extent_y, 4:4 + extent_z]
        neighbours = neighbours + padded[4:4 + extent_x, 4:4 + extent_y, 4 + offset:4 + offset + extent_z] + padded[4:4 + extent_x, 4:4 + extent_y, 4 - offset:4 - offset + extent_z]
        accumulated = accumulated + STENCIL_WEIGHTS[offset] * neighbours
    return accumulated


def group_term(velocity, aperture_rows, source_index, wave_row, trace_rows, receiver_rows, start_index, forward_previous, forward_current, adjoint_next, adjoint_current):
    chosen_tiles = velocity[aperture_rows]
    speed = chosen_tiles.transpose(0, 2, 1, 3, 4).reshape(NXA, AY, TZ)
    courant = (STEP_SCALE * speed) ** 2
    amplitudes = lax.dynamic_slice_in_dim(wave_row, start_index.astype(jnp.int32), STEPS, 0)
    recorded = lax.dynamic_slice_in_dim(trace_rows, start_index.astype(jnp.int32), STEPS, 0)
    forward_fields = [forward_previous, forward_current]
    for moment in range(STEPS):
        present = forward_fields[-1]
        padded_x = jnp.pad(present, ((4, 4), (0, 0), (0, 0)))
        advanced = 2.0 * present - forward_fields[-2] + courant * laplace(present, padded_x)
        advanced = advanced.reshape(-1).at[source_index].add(amplitudes[moment]).reshape(present.shape)
        forward_fields.append(advanced)
    misfits = {}
    for moment in range(1, STEPS + 1):
        misfits[moment] = forward_fields[moment + 1].reshape(-1)[receiver_rows] - recorded[moment - 1]
    later = adjoint_next
    present = adjoint_current
    imaging = jnp.zeros_like(speed)
    for moment in range(STEPS, 0, -1):
        padded_x = jnp.pad(present, ((4, 4), (0, 0), (0, 0)))
        earlier = 2.0 * present - later + courant * laplace(present, padded_x)
        earlier = earlier.reshape(-1).at[receiver_rows].add(misfits[moment]).reshape(present.shape)
        index_n = moment - 1
        curvature = forward_fields[index_n + 2] - 2.0 * forward_fields[index_n + 1] + forward_fields[index_n]
        imaging = imaging + earlier * curvature
        later = present
        present = earlier
    gradient_term = 2.0 / speed ** 3 * imaging
    return gradient_term.reshape(SLABS, TX, APER, TY, TZ).transpose(0, 2, 1, 3, 4)


def reference(velocity, aperture, source_cell, wavelet, observed, receivers, checkpoint, forward_previous, forward_current, adjoint_next, adjoint_current):
    def scan_group(carried, inputs):
        aperture_rows, source_index, wave_row, trace_rows, receiver_rows, start_index, f_prev, f_cur, a_next, a_cur = inputs
        gradient_term = group_term(velocity, aperture_rows, source_index, wave_row, trace_rows, receiver_rows, start_index, f_prev, f_cur, a_next, a_cur)
        carried = carried.at[aperture_rows.reshape(-1)].add(gradient_term.reshape(SLABS * APER, TX, TY, TZ))
        return carried, None

    initial = jnp.zeros((TILES, TX, TY, TZ), jnp.float32)
    result, unused = lax.scan(scan_group, initial, (aperture, source_cell, wavelet, observed, receivers, checkpoint, forward_previous, forward_current, adjoint_next, adjoint_current))
    return result
```

```python
import jax
import jax.numpy as jnp
from jax import lax
from jax.experimental import pallas as pl
from jax.experimental.pallas import tpu as pltpu
from jax.sharding import Mesh, PartitionSpec as P

STEPS = 8
STENCIL_WEIGHTS = (-205.0 / 72.0, 8.0 / 5.0, -1.0 / 5.0, 8.0 / 315.0, -1.0 / 560.0)
STEP_SCALE = 0.088
DOM = ("yl", "z", "c")
SHOT = ("x", "yh")
SLABS = 32
TX, AY, TZ = 8, 16, 128
PLANES = 9 * TX
OWN = 4 * TX
PAD = 8
NREC = 256


def laplace_plane(field, cur, p, lane):
    middle = field[cur, p, PAD : PAD + AY, :]
    acc = (3.0 * STENCIL_WEIGHTS[0]) * middle
    for s in range(1, 5):
        near = field[cur, p + s, PAD : PAD + AY, :] + field[cur, p - s, PAD : PAD + AY, :]
        near = near + field[cur, p, PAD + s : PAD + AY + s, :] + field[cur, p, PAD - s : PAD + AY - s, :]
        near = near + jnp.where(lane < TZ - s, pltpu.roll(middle, TZ - s, 1), 0.0)
        near = near + jnp.where(lane >= s, pltpu.roll(middle, s, 1), 0.0)
        acc = acc + STENCIL_WEIGHTS[s] * near
    return middle, acc


def assemble(field, which, item, slab, own, left, right, far_left, far_right):
    pieces = [far_left[k, item] for k in range(3)] + [left[item], own[item], right[item]] + [far_right[k, item] for k in range(3)]
    for j in range(9):
        there = slab + (j - 4)
        inside = (there >= 0) & (there < SLABS)
        field[which, TX * j : TX * (j + 1), PAD : PAD + AY, :] = jnp.where(inside, pieces[j], 0.0)


def clear_pads(field):
    zero = jnp.zeros((PLANES, PAD, TZ), jnp.float32)
    for b in range(2):
        field[b, :, 0:PAD, :] = zero
        field[b, :, PAD + AY : PAD + AY + PAD, :] = zero


def split3(x):
    high = x.astype(jnp.bfloat16)
    rest = x - high.astype(jnp.float32)
    mid = rest.astype(jnp.bfloat16)
    low = (rest - mid.astype(jnp.float32)).astype(jnp.bfloat16)
    return high, mid, low


def forward_kernel(
    aperture, source, checkpoint, wavelet, observed, receivers,
    own, left, right, far_left, far_right,
    vel, vel_left, vel_right, vel_far_left, vel_far_right,
    curvature, misfit, courant,
    field, update, samples,
):
    slab = aperture[0, 0, 0] & (SLABS - 1)
    clear_pads(field)
    for item in range(2):
        assemble(field, item, item, slab, own, left, right, far_left, far_right)
    tiles = (
        [(vel_far_left, k) for k in range(3)] + [(vel_left, None), (vel, None), (vel_right, None)] + [(vel_far_right, k) for k in range(3)]
    )
    for j in range(9):
        there = slab + (j - 4)
        inside = (there >= 0) & (there < SLABS)
        ref, k = tiles[j]
        for row in range(2):
            speed = ref[row] if k is None else ref[k, row]
            speed = jnp.where(inside, STEP_SCALE * speed, 0.0)
            courant[TX * j : TX * (j + 1), 8 * row : 8 * row + 8, :] = speed * speed

    lane = lax.broadcasted_iota(jnp.int32, (AY, TZ), 1)
    suby = lax.broadcasted_iota(jnp.int32, (AY, TZ), 0)
    cell = source[0]
    source_x = (cell >> 11) - (slab - 4) * TX
    source_here = (source_x >= 0) & (source_x < PLANES)
    source_own = (source_x >= OWN) & (source_x < OWN + TX)
    spot = (suby == ((cell >> 7) & 15)) & (lane == (cell & 127))
    start = checkpoint[0]

    def step(n, _):
        prev = n & 1
        cur = 1 - prev

        def planes(b, _):
            for q in range(4):
                p = 4 * b + q
                middle, acc = laplace_plane(field, cur, p, lane)
                change = courant[p] * acc
                update[p] = change
                field[prev, p, PAD : PAD + AY, :] = 2.0 * middle - field[prev, p, PAD : PAD + AY, :] + change
            return 0

        lax.fori_loop(1 + n, 17 - n, planes, 0)
        pulse = jnp.where(spot, wavelet[0, start + n], 0.0)

        @pl.when(source_here)
        def _():
            field[prev, source_x, PAD : PAD + AY, :] = field[prev, source_x, PAD : PAD + AY, :] + pulse

        @pl.when(source_own)
        def _():
            update[source_x] = update[source_x] + pulse

        curvature[n] = update[OWN : OWN + TX]
        samples[n] = field[prev, OWN : OWN + TX, PAD : PAD + AY, :].reshape(TX * AY, TZ)
        return 0

    lax.fori_loop(0, STEPS, step, 0)

    spots = receivers[...]
    row = (spots >> 7) - slab * (TX * AY)
    rows = lax.broadcasted_iota(jnp.int32, (TX * AY, NREC), 0)
    at_row = jnp.where(rows == row, 1.0, 0.0)
    at_lane = jnp.where(rows == (spots & 127), 1.0, 0.0).astype(jnp.bfloat16)
    here = (row >= 0) & (row < TX * AY)
    taken = []
    for n in range(STEPS):
        total = None
        for part in split3(samples[n]):
            product = jnp.dot(part, at_lane, preferred_element_type=jnp.float32)
            total = product if total is None else total + product
        recorded = observed[0, pl.ds(start + n, 1), :]
        taken.append(jnp.sum(total * at_row, axis=0, keepdims=True) - jnp.where(here, recorded, 0.0))
    misfit[...] = jnp.concatenate(taken, axis=0)


def adjoint_kernel(
    aperture, receivers, misfit_near, misfit_left, misfit_right,
    own, left, right, far_left, far_right,
    vel, courant, curvature,
    out,
    field, injected, image,
):
    slab = aperture[0, 0, 0] & (SLABS - 1)
    first_row = aperture[0, 0, 0] >> 5
    clear_pads(field)
    for item in range(2):
        assemble(field, item, item, slab, own, left, right, far_left, far_right)
    lane = lax.broadcasted_iota(jnp.int32, (AY, TZ), 1)
    misfit = misfit_near[...] + misfit_left[...] + misfit_right[...]
    spots = receivers[...]
    row = (spots >> 7) - (slab - 4) * (TX * AY)
    rows = lax.broadcasted_iota(jnp.int32, (PLANES * AY, NREC), 0)
    at_row = jnp.where(rows == row, 1.0, 0.0).astype(jnp.bfloat16)
    at_lane = rows[0:TZ] == (spots & 127)
    image[...] = jnp.zeros((TX, AY, TZ), jnp.float32)
    for i in range(STEPS):
        n = STEPS - i
        prev, cur = i & 1, 1 - (i & 1)
        low, high = 4 + 4 * i, PLANES - 4 - 4 * i
        parts = [jnp.where(at_lane, part.astype(jnp.float32), 0.0).astype(jnp.bfloat16) for part in split3(misfit[n - 1 : n])]
        total = None
        for part in parts:
            product = lax.dot_general(
                at_row[low * AY : high * AY], part, (((1,), (1,)), ((), ())), preferred_element_type=jnp.float32
            )
            total = product if total is None else total + product
        injected[low:high] = total.reshape(high - low, AY, TZ)

        def planes(b, _, prev=prev, cur=cur):
            for q in range(4):
                p = 4 * b + q
                middle, acc = laplace_plane(field, cur, p, lane)
                field[prev, p, PAD : PAD + AY, :] = (
                    2.0 * middle - field[prev, p, PAD : PAD + AY, :] + courant[p] * acc + injected[p]
                )
            return 0

        lax.fori_loop(low // 4, high // 4, planes, 0)
        image[...] += field[prev, OWN : OWN + TX, PAD : PAD + AY, :] * curvature[n - 1]
    out[...] = jnp.zeros(out.shape, jnp.float32)
    for k in range(2):
        speed = vel[k]
        out[first_row + k] = 2.0 / (speed * speed * speed) * image[:, 8 * k : 8 * k + 8, :]


def whole(shape):
    return pl.BlockSpec(shape, lambda i: (0,) * len(shape))


def pair(shape, which):
    place = len(shape) - 4
    return pl.BlockSpec(shape, lambda i: tuple(which if k == place else 0 for k in range(len(shape))))


def scalars(shape):
    return pl.BlockSpec(shape, lambda i: (0,) * len(shape), memory_space=pltpu.SMEM)


def fields_specs(which):
    near, far = (2, TX, AY, TZ), (3, 2, TX, AY, TZ)
    return [pair(near, which)] * 3 + [pair(far, which)] * 2


def body(
    velocity,
    aperture,
    source_cell,
    wavelet,
    observed,
    receivers,
    checkpoint,
    forward_previous,
    forward_current,
    adjoint_next,
    adjoint_current,
):
    def shift(cells, by):
        return lax.ppermute(cells, DOM, [(i, (i + by) % SLABS) for i in range(SLABS)])

    fields = jnp.concatenate([forward_previous, forward_current, adjoint_next, adjoint_current], axis=0)
    left, right = shift(fields, 1), shift(fields, -1)

    column = lax.all_to_all(jnp.broadcast_to(velocity, (4,) + velocity.shape[1:]), "yh", 0, 0, tiled=True)

    packed = jnp.stack([left, fields, right])
    far_left, far_right = shift(packed, 3), shift(packed, -3)

    rows = lax.all_to_all(jnp.broadcast_to(column[None], (4,) + column.shape), "x", 0, 0, tiled=True)
    rows = rows.reshape((16,) + velocity.shape[1:])
    vel = lax.dynamic_slice_in_dim(rows, aperture[0, 0, 0] // SLABS, 2, 0)
    vel_left, vel_right = shift(vel, 1), shift(vel, -1)
    vel_packed = jnp.stack([vel_left, vel, vel_right])
    vel_far_left, vel_far_right = shift(vel_packed, 3), shift(vel_packed, -3)

    tile, tiles = (2, TX, 8, TZ), (3, 2, TX, 8, TZ)
    slab_steps = (STEPS, TX, AY, TZ)
    region = (PLANES, AY, TZ)
    f32 = jnp.float32
    curvature, misfit, courant = pl.pallas_call(
        forward_kernel,
        grid=(1,),
        in_specs=[scalars((1, 1, 2)), scalars((1,)), scalars((1,)), scalars((1, 64)), whole((1, 64, NREC)), whole((1, NREC))]
        + fields_specs(0)
        + [whole(tile)] * 3
        + [whole(tiles)] * 2,
        out_specs=[whole(slab_steps), whole((STEPS, NREC)), whole(region)],
        out_shape=[
            jax.ShapeDtypeStruct(slab_steps, f32),
            jax.ShapeDtypeStruct((STEPS, NREC), f32),
            jax.ShapeDtypeStruct(region, f32),
        ],
        scratch_shapes=[
            pltpu.VMEM((2, PLANES, AY + 2 * PAD, TZ), f32),
            pltpu.VMEM(region, f32),
            pltpu.VMEM((STEPS, TX * AY, TZ), f32),
        ],
        name="forward",
    )(
        aperture, source_cell, checkpoint, wavelet, observed, receivers,
        fields, left, right, far_left, far_right,
        vel, vel_left, vel_right, vel_far_left, vel_far_right,
    )

    near = misfit + shift(misfit, 1) + shift(misfit, -1)
    misfit_left, misfit_right = shift(near, 3), shift(near, -3)

    slots = (16, TX, 8, TZ)
    terms = pl.pallas_call(
        adjoint_kernel,
        grid=(1,),
        in_specs=[scalars((1, 1, 2)), whole((1, NREC))]
        + [whole((STEPS, NREC))] * 3
        + fields_specs(1)
        + [whole(tile), whole(region), whole(slab_steps)],
        out_specs=whole(slots),
        out_shape=jax.ShapeDtypeStruct(slots, f32),
        scratch_shapes=[
            pltpu.VMEM((2, PLANES, AY + 2 * PAD, TZ), f32),
            pltpu.VMEM(region, f32),
            pltpu.VMEM((TX, AY, TZ), f32),
        ],
        name="adjoint",
    )(
        aperture, receivers, near, misfit_left, misfit_right,
        fields, left, right, far_left, far_right,
        vel, courant, curvature,
    )
    landed = lax.all_to_all(terms, SHOT, 0, 0, tiled=True)
    return jnp.sum(landed, axis=0, keepdims=True)


def solution(mesh):
    split = Mesh(mesh.devices.reshape(4, 4, 2, 8, 2), SHOT + DOM)
    placed = (
        P(SHOT + DOM, None, None, None),
        P(SHOT, DOM, None),
        P(SHOT),
        P(SHOT, None),
        P(SHOT, None, None),
        P(SHOT, None),
        P(SHOT),
        P(SHOT, DOM, None, None),
        P(SHOT, DOM, None, None),
        P(SHOT, DOM, None, None),
        P(SHOT, DOM, None, None),
    )
    return jax.shard_map(
        body,
        mesh=split,
        in_specs=placed,
        out_specs=P(SHOT + DOM, None, None, None),
        check_vma=False,
    )
```

```python
import jax
import jax.numpy as jnp
from jax import lax
from jax.experimental import pallas as pl
from jax.experimental.pallas import tpu as pltpu
from jax.sharding import Mesh, PartitionSpec as P

STEPS = 8
STENCIL_WEIGHTS = (-205.0 / 72.0, 8.0 / 5.0, -1.0 / 5.0, 8.0 / 315.0, -1.0 / 560.0)
STEP_SCALE = 0.088
DOM = ("yl", "z", "c")
SHOT = ("x", "yh")
SLABS = 32
TX, AY, TZ = 8, 16, 128
PLANES = 9 * TX
OWN = 4 * TX
PAD = 8
NREC = 256


def split2(x):
    high = x.astype(jnp.bfloat16)
    return high, (x - high.astype(jnp.float32)).astype(jnp.bfloat16)


def along_z():
    apart = jnp.abs(
        lax.broadcasted_iota(jnp.int32, (TZ, TZ), 0) - lax.broadcasted_iota(jnp.int32, (TZ, TZ), 1)
    )
    band = jnp.where(apart == 0, 3.0 * STENCIL_WEIGHTS[0], 0.0)
    for s in range(1, 5):
        band = jnp.where(apart == s, STENCIL_WEIGHTS[s], band)
    high, low = split2(band)
    top = jnp.concatenate([high, low], axis=1)
    return jnp.concatenate([top, jnp.concatenate([high, jnp.zeros_like(low)], axis=1)], axis=0)


def stack_parts(x):
    return jnp.concatenate(split2(x), axis=1)


def halves(product):
    return product[:, :TZ] + product[:, TZ:]


def z_pass(field, cur, matrix, low, high, zpart):
    for p in range(low, high, 16):
        q = min(p + 16, high)
        rows = field[cur, p:q, PAD : PAD + AY, :].reshape((q - p) * AY, TZ)
        product = jnp.dot(stack_parts(rows), matrix[...], preferred_element_type=jnp.float32)
        zpart[p:q] = halves(product).reshape(q - p, AY, TZ)


def xy_block(field, cur, p, h, zpart):
    y = PAD + 8 * h
    column = field[cur, pl.ds(p - 4, 16), y : y + 8, :]
    acc = zpart[pl.ds(p, 8), 8 * h : 8 * h + 8, :]
    for s in range(1, 5):
        near = column[4 + s : 12 + s] + column[4 - s : 12 - s]
        near = near + (field[cur, pl.ds(p, 8), y + s : y + 8 + s, :] + field[cur, pl.ds(p, 8), y - s : y + 8 - s, :])
        acc = acc + STENCIL_WEIGHTS[s] * near
    return column[4:12], acc


def assemble(field, which, item, slab, own, other, near, far, swapped_near, swapped_far):
    def put(j, value):
        there = slab + j
        inside = (there >= 0) & (there < SLABS)
        field[which, TX * (j + 4) : TX * (j + 5), PAD : PAD + AY, :] = jnp.where(inside, value, 0.0)

    put(0, own[item])

    @pl.when((slab & 1) == 0)
    def _():
        put(-4, far[0, item])
        put(-3, far[1, item])
        put(-2, near[0, item])
        put(-1, near[1, item])
        put(1, other[item])
        put(2, swapped_near[1, item])
        put(3, swapped_near[0, item])
        put(4, swapped_far[1, item])

    @pl.when((slab & 1) == 1)
    def _():
        put(-4, swapped_far[1, item])
        put(-3, swapped_near[0, item])
        put(-2, swapped_near[1, item])
        put(-1, other[item])
        put(1, near[1, item])
        put(2, near[0, item])
        put(3, far[1, item])
        put(4, far[0, item])


def clear_pads(field):
    zero = jnp.zeros((PLANES, PAD, TZ), jnp.float32)
    for b in range(2):
        field[b, :, 0:PAD, :] = zero
        field[b, :, PAD + AY : PAD + AY + PAD, :] = zero


def forward_kernel(
    aperture, source, checkpoint, wavelet, observed, receivers,
    own, other, near, far, swapped_near, swapped_far,
    vel, vel_left, vel_right, vel_far_left, vel_far_right,
    curvature, misfit, courant,
    field, update, samples, zpart, matrix,
):
    slab = aperture[0, 0, 0] & (SLABS - 1)
    clear_pads(field)
    matrix[...] = along_z()
    for item in range(2):
        assemble(field, item, item, slab, own, other, near, far, swapped_near, swapped_far)
    tiles = (
        [(vel_far_left, k) for k in range(3)] + [(vel_left, None), (vel, None), (vel_right, None)] + [(vel_far_right, k) for k in range(3)]
    )
    for j in range(9):
        there = slab + (j - 4)
        inside = (there >= 0) & (there < SLABS)
        ref, k = tiles[j]
        for row in range(2):
            speed = ref[row] if k is None else ref[k, row]
            speed = jnp.where(inside, STEP_SCALE * speed, 0.0)
            courant[TX * j : TX * (j + 1), 8 * row : 8 * row + 8, :] = speed * speed

    lane = lax.broadcasted_iota(jnp.int32, (AY, TZ), 1)
    suby = lax.broadcasted_iota(jnp.int32, (AY, TZ), 0)
    cell = source[0]
    source_x = (cell >> 11) - (slab - 4) * TX
    source_here = (source_x >= 0) & (source_x < PLANES)
    source_own = (source_x >= OWN) & (source_x < OWN + TX)
    spot = (suby == ((cell >> 7) & 15)) & (lane == (cell & 127))
    start = checkpoint[0]

    for n in range(STEPS):
        prev, cur = n & 1, 1 - (n & 1)
        low, high = 4 + 4 * n, PLANES - 4 - 4 * n
        z_pass(field, cur, matrix, low, high, zpart)

        def planes(b, _, prev=prev, cur=cur, low=low):
            p = low + 8 * b
            for h in range(2):
                y = PAD + 8 * h
                middle, acc = xy_block(field, cur, p, h, zpart)
                change = courant[pl.ds(p, 8), 8 * h : 8 * h + 8, :] * acc
                update[pl.ds(p, 8), 8 * h : 8 * h + 8, :] = change
                field[prev, pl.ds(p, 8), y : y + 8, :] = (middle + middle) - field[prev, pl.ds(p, 8), y : y + 8, :] + change
            return 0

        lax.fori_loop(0, (high - low) // 8, planes, 0)
        pulse = jnp.where(spot, wavelet[0, start + n], 0.0)

        @pl.when(source_here)
        def _(prev=prev, pulse=pulse):
            field[prev, source_x, PAD : PAD + AY, :] = field[prev, source_x, PAD : PAD + AY, :] + pulse

        @pl.when(source_own)
        def _(pulse=pulse):
            update[source_x] = update[source_x] + pulse

        curvature[n] = update[OWN : OWN + TX]
        samples[n] = field[prev, OWN : OWN + TX, PAD : PAD + AY, :].reshape(TX * AY, TZ)

    spots = receivers[...]
    row = (spots >> 7) - slab * (TX * AY)
    rows = lax.broadcasted_iota(jnp.int32, (TX * AY, NREC), 0)
    at_row = jnp.where(rows == row, 1.0, 0.0)
    at_lane = jnp.where(rows == (spots & 127), 1.0, 0.0).astype(jnp.bfloat16)
    at_lane = jnp.concatenate([at_lane, at_lane], axis=0)
    here = (row >= 0) & (row < TX * AY)
    taken = []
    for n in range(STEPS):
        product = jnp.dot(stack_parts(samples[n]), at_lane, preferred_element_type=jnp.float32)
        recorded = observed[0, pl.ds(start + n, 1), :]
        taken.append(jnp.sum(product * at_row, axis=0, keepdims=True) - jnp.where(here, recorded, 0.0))
    misfit[...] = jnp.concatenate(taken, axis=0)


def adjoint_kernel(
    aperture, receivers, misfit_near, misfit_left, misfit_right,
    own, other, near, far, swapped_near, swapped_far,
    vel, courant, curvature,
    out,
    field, injected, image, zpart, matrix, at_row,
):
    slab = aperture[0, 0, 0] & (SLABS - 1)
    first_row = aperture[0, 0, 0] >> 5
    clear_pads(field)
    matrix[...] = along_z()
    for item in range(2):
        assemble(field, item, 2 + item, slab, own, other, near, far, swapped_near, swapped_far)
    misfit = misfit_near[...] + misfit_left[...] + misfit_right[...]
    spots = receivers[...]
    row = (spots >> 7) - (slab - 4) * (TX * AY)
    rows = lax.broadcasted_iota(jnp.int32, (PLANES * AY, NREC), 0)
    at_row[...] = jnp.where(rows == row, 1.0, 0.0).astype(jnp.bfloat16)
    at_lane = rows[0:TZ] == (spots & 127)
    image[...] = jnp.zeros((TX, AY, TZ), jnp.float32)
    for i in range(STEPS):
        n = STEPS - i
        prev, cur = i & 1, 1 - (i & 1)
        low, high = 4 + 4 * i, PLANES - 4 - 4 * i
        parts = [jnp.where(at_lane, part.astype(jnp.float32), 0.0).astype(jnp.bfloat16) for part in split2(misfit[n - 1 : n])]
        sent = jnp.concatenate(parts, axis=0)
        for p in range(low, high, 16):
            q = min(p + 16, high)
            product = lax.dot_general(
                at_row[p * AY : q * AY], sent, (((1,), (1,)), ((), ())), preferred_element_type=jnp.float32
            )
            injected[p:q] = halves(product).reshape(q - p, AY, TZ)
        z_pass(field, cur, matrix, low, high, zpart)

        def planes(b, _, prev=prev, cur=cur, low=low):
            p = low + 8 * b
            for h in range(2):
                y = PAD + 8 * h
                middle, acc = xy_block(field, cur, p, h, zpart)
                change = courant[pl.ds(p, 8), 8 * h : 8 * h + 8, :] * acc + injected[pl.ds(p, 8), 8 * h : 8 * h + 8, :]
                field[prev, pl.ds(p, 8), y : y + 8, :] = (middle + middle) - field[prev, pl.ds(p, 8), y : y + 8, :] + change
            return 0

        lax.fori_loop(0, (high - low) // 8, planes, 0)
        image[...] += field[prev, OWN : OWN + TX, PAD : PAD + AY, :] * curvature[n - 1]
    out[...] = jnp.zeros(out.shape, jnp.float32)
    for k in range(2):
        speed = vel[k]
        out[first_row + k] = 2.0 / (speed * speed * speed) * image[:, 8 * k : 8 * k + 8, :]


def in_vmem(count):
    return [pl.BlockSpec(memory_space=pltpu.VMEM)] * count


def in_smem(count):
    return [pl.BlockSpec(memory_space=pltpu.SMEM)] * count


def body(
    velocity,
    aperture,
    source_cell,
    wavelet,
    observed,
    receivers,
    checkpoint,
    forward_previous,
    forward_current,
    adjoint_next,
    adjoint_current,
):
    def shift(cells, by):
        return lax.ppermute(cells, DOM, [(i, (i + by) % SLABS) for i in range(SLABS)])

    def partner(cells):
        return lax.ppermute(cells, DOM, [(i, i ^ 1) for i in range(SLABS)])

    def next_chip(cells):
        return lax.ppermute(cells, DOM, [(i, (i + (-2 if i % 2 else 2)) % SLABS) for i in range(SLABS)])

    own = jnp.concatenate([forward_previous, forward_current, adjoint_next, adjoint_current], axis=0)
    other = partner(own)
    column = lax.all_to_all(
        jnp.broadcast_to(velocity[None], (4,) + velocity.shape), "yh", 0, 0, tiled=True
    )
    near = next_chip(jnp.stack([own, other]))
    rows = lax.all_to_all(jnp.broadcast_to(column[None], (4,) + column.shape), "x", 0, 0, tiled=True)
    far = next_chip(near)
    swapped_near, swapped_far = partner(near), partner(far)
    fields = (own, other, near, far, swapped_near, swapped_far)

    rows = rows.reshape((16,) + velocity.shape[1:])
    vel = lax.dynamic_slice_in_dim(rows, aperture[0, 0, 0] // SLABS, 2, 0)
    vel_left, vel_right = shift(vel, 1), shift(vel, -1)
    vel_packed = jnp.stack([vel_left, vel, vel_right])
    vel_far_left, vel_far_right = shift(vel_packed, 3), shift(vel_packed, -3)

    slab_steps = (STEPS, TX, AY, TZ)
    region = (PLANES, AY, TZ)
    f32 = jnp.float32
    padded = pltpu.VMEM((2, PLANES, AY + 2 * PAD, TZ), f32)
    matrix = pltpu.VMEM((2 * TZ, 2 * TZ), jnp.bfloat16)
    limit = pltpu.CompilerParams(vmem_limit_bytes=32 << 20)
    curvature, misfit, courant = pl.pallas_call(
        forward_kernel,
        in_specs=in_smem(4) + in_vmem(13),
        out_specs=in_vmem(3),
        out_shape=[
            jax.ShapeDtypeStruct(slab_steps, f32),
            jax.ShapeDtypeStruct((STEPS, NREC), f32),
            jax.ShapeDtypeStruct(region, f32),
        ],
        scratch_shapes=[
            padded,
            pltpu.VMEM(region, f32),
            pltpu.VMEM((STEPS, TX * AY, TZ), f32),
            pltpu.VMEM(region, f32),
            matrix,
        ],
        compiler_params=limit,
        name="forward",
    )(
        aperture, source_cell, checkpoint, wavelet, observed, receivers, *fields,
        vel, vel_left, vel_right, vel_far_left, vel_far_right,
    )

    near = misfit + shift(misfit, 1) + shift(misfit, -1)
    misfit_left, misfit_right = shift(near, 3), shift(near, -3)

    terms = pl.pallas_call(
        adjoint_kernel,
        in_specs=in_smem(1) + in_vmem(13),
        out_specs=in_vmem(1)[0],
        out_shape=jax.ShapeDtypeStruct((16, TX, 8, TZ), f32),
        scratch_shapes=[
            padded,
            pltpu.VMEM(region, f32),
            pltpu.VMEM((TX, AY, TZ), f32),
            pltpu.VMEM(region, f32),
            matrix,
            pltpu.VMEM((PLANES * AY, NREC), jnp.bfloat16),
        ],
        compiler_params=limit,
        name="adjoint",
    )(
        aperture, receivers, near, misfit_left, misfit_right, *fields,
        vel, courant, curvature,
    )
    landed = lax.all_to_all(terms, SHOT, 0, 0, tiled=True)
    return jnp.sum(landed, axis=0, keepdims=True)


def solution(mesh):
    split = Mesh(mesh.devices.reshape(4, 4, 2, 8, 2), SHOT + DOM)
    placed = (
        P(SHOT + DOM, None, None, None),
        P(SHOT, DOM, None),
        P(SHOT),
        P(SHOT, None),
        P(SHOT, None, None),
        P(SHOT, None),
        P(SHOT),
        P(SHOT, DOM, None, None),
        P(SHOT, DOM, None, None),
        P(SHOT, DOM, None, None),
        P(SHOT, DOM, None, None),
    )
    return jax.shard_map(
        body,
        mesh=split,
        in_specs=placed,
        out_specs=P(SHOT + DOM, None, None, None),
        check_vma=False,
    )
```

```python
import jax
import jax.numpy as jnp
from jax import lax
from jax.experimental import pallas as pl
from jax.experimental.pallas import tpu as pltpu
from jax.sharding import Mesh, PartitionSpec as P


STEPS = 8
STENCIL_WEIGHTS = (-205.0 / 72.0, 8.0 / 5.0, -1.0 / 5.0, 8.0 / 315.0, -1.0 / 560.0)
STEP_SCALE = 0.088
DOM = ("yl", "z", "c")
SHOT = ("x", "yh")
SLABS = 32
TX, AY, TZ = 8, 16, 128
PLANES = 9 * TX
OWN = 4 * TX
PAD = 8
NREC = 256


def split2(x):
    high = x.astype(jnp.bfloat16)
    return high, (x - high.astype(jnp.float32)).astype(jnp.bfloat16)


def along_z():
    apart = jnp.abs(
        lax.broadcasted_iota(jnp.int32, (TZ, TZ), 0) - lax.broadcasted_iota(jnp.int32, (TZ, TZ), 1)
    )
    band = jnp.where(apart == 0, 3.0 * STENCIL_WEIGHTS[0], 0.0)
    for s in range(1, 5):
        band = jnp.where(apart == s, STENCIL_WEIGHTS[s], band)
    high, low = split2(band)
    top = jnp.concatenate([high, low], axis=1)
    return jnp.concatenate([top, jnp.concatenate([high, jnp.zeros_like(low)], axis=1)], axis=0)


def stack_parts(x):
    return jnp.concatenate(split2(x), axis=1)


def halves(product):
    return product[:, :TZ] + product[:, TZ:]


def z_pass(field, cur, matrix, low, high, zpart):
    for p in range(low, high, 16):
        q = min(p + 16, high)
        rows = field[cur, p:q, PAD : PAD + AY, :].reshape((q - p) * AY, TZ)
        product = jnp.dot(stack_parts(rows), matrix[...], preferred_element_type=jnp.float32)
        zpart[p:q] = halves(product).reshape(q - p, AY, TZ)


def xy_block(field, cur, p, h, zpart):
    y = PAD + 8 * h
    column = field[cur, pl.ds(p - 4, 16), y : y + 8, :]
    acc = zpart[pl.ds(p, 8), 8 * h : 8 * h + 8, :]
    for s in range(1, 5):
        near = column[4 + s : 12 + s] + column[4 - s : 12 - s]
        near = near + (field[cur, pl.ds(p, 8), y + s : y + 8 + s, :] + field[cur, pl.ds(p, 8), y - s : y + 8 - s, :])
        acc = acc + STENCIL_WEIGHTS[s] * near
    return column[4:12], acc


def assemble(field, which, item, slab, own, other, near, far, swapped_near, swapped_far):
    def put(j, value):
        there = slab + j
        inside = (there >= 0) & (there < SLABS)
        field[which, TX * (j + 4) : TX * (j + 5), PAD : PAD + AY, :] = jnp.where(inside, value, 0.0)

    put(0, own[item])

    @pl.when((slab & 1) == 0)
    def _():
        put(-4, far[0, item])
        put(-3, far[1, item])
        put(-2, near[0, item])
        put(-1, near[1, item])
        put(1, other[item])
        put(2, swapped_near[1, item])
        put(3, swapped_near[0, item])
        put(4, swapped_far[1, item])

    @pl.when((slab & 1) == 1)
    def _():
        put(-4, swapped_far[1, item])
        put(-3, swapped_near[0, item])
        put(-2, swapped_near[1, item])
        put(-1, other[item])
        put(1, near[1, item])
        put(2, near[0, item])
        put(3, far[1, item])
        put(4, far[0, item])


def clear_pads(field):
    zero = jnp.zeros((PLANES, PAD, TZ), jnp.float32)
    for b in range(2):
        field[b, :, 0:PAD, :] = zero
        field[b, :, PAD + AY : PAD + AY + PAD, :] = zero


def forward_kernel(
    aperture, source, checkpoint, wavelet, observed, receivers,
    own, other, near, far, swapped_near, swapped_far,
    vel, vel_left, vel_right, vel_far_left, vel_far_right,
    curvature, misfit, courant,
    field, update, samples, zpart, matrix,
):
    slab = aperture[0, 0, 0] & (SLABS - 1)
    clear_pads(field)
    matrix[...] = along_z()
    for item in range(2):
        assemble(field, item, item, slab, own, other, near, far, swapped_near, swapped_far)
    tiles = (
        [(vel_far_left, k) for k in range(3)] + [(vel_left, None), (vel, None), (vel_right, None)] + [(vel_far_right, k) for k in range(3)]
    )
    for j in range(9):
        there = slab + (j - 4)
        inside = (there >= 0) & (there < SLABS)
        ref, k = tiles[j]
        for row in range(2):
            speed = ref[row] if k is None else ref[k, row]
            speed = jnp.where(inside, STEP_SCALE * speed, 0.0)
            courant[TX * j : TX * (j + 1), 8 * row : 8 * row + 8, :] = speed * speed

    lane = lax.broadcasted_iota(jnp.int32, (AY, TZ), 1)
    suby = lax.broadcasted_iota(jnp.int32, (AY, TZ), 0)
    cell = source[0]
    source_x = (cell >> 11) - (slab - 4) * TX
    source_here = (source_x >= 0) & (source_x < PLANES)
    source_own = (source_x >= OWN) & (source_x < OWN + TX)
    spot = (suby == ((cell >> 7) & 15)) & (lane == (cell & 127))
    start = checkpoint[0]

    for n in range(STEPS):
        prev, cur = n & 1, 1 - (n & 1)
        low, high = 4 + 4 * n, PLANES - 4 - 4 * n
        z_pass(field, cur, matrix, low, high, zpart)

        def planes(b, _, prev=prev, cur=cur, low=low):
            p = low + 8 * b
            for h in range(2):
                y = PAD + 8 * h
                middle, acc = xy_block(field, cur, p, h, zpart)
                change = courant[pl.ds(p, 8), 8 * h : 8 * h + 8, :] * acc
                update[pl.ds(p, 8), 8 * h : 8 * h + 8, :] = change
                field[prev, pl.ds(p, 8), y : y + 8, :] = (middle + middle) - field[prev, pl.ds(p, 8), y : y + 8, :] + change
            return 0

        lax.fori_loop(0, (high - low) // 8, planes, 0)
        pulse = jnp.where(spot, wavelet[0, start + n], 0.0)

        @pl.when(source_here)
        def _(prev=prev, pulse=pulse):
            field[prev, source_x, PAD : PAD + AY, :] = field[prev, source_x, PAD : PAD + AY, :] + pulse

        @pl.when(source_own)
        def _(pulse=pulse):
            update[source_x] = update[source_x] + pulse

        curvature[n] = update[OWN : OWN + TX]
        samples[n] = field[prev, OWN : OWN + TX, PAD : PAD + AY, :].reshape(TX * AY, TZ)

    spots = receivers[...]
    row = (spots >> 7) - slab * (TX * AY)
    rows = lax.broadcasted_iota(jnp.int32, (TX * AY, NREC), 0)
    at_row = jnp.where(rows == row, 1.0, 0.0)
    at_lane = jnp.where(rows == (spots & 127), 1.0, 0.0).astype(jnp.bfloat16)
    at_lane = jnp.concatenate([at_lane, at_lane], axis=0)
    here = (row >= 0) & (row < TX * AY)
    taken = []
    for n in range(STEPS):
        product = jnp.dot(stack_parts(samples[n]), at_lane, preferred_element_type=jnp.float32)
        recorded = observed[0, pl.ds(start + n, 1), :]
        taken.append(jnp.sum(product * at_row, axis=0, keepdims=True) - jnp.where(here, recorded, 0.0))
    found = jnp.concatenate(taken, axis=0)
    for k in range(SLABS):
        misfit[k] = found


def adjoint_kernel(
    aperture, receivers, misfits,
    own, other, near, far, swapped_near, swapped_far,
    vel, courant, curvature,
    out,
    field, injected, image, zpart, matrix, at_row,
):
    slab = aperture[0, 0, 0] & (SLABS - 1)
    first_row = aperture[0, 0, 0] >> 5
    clear_pads(field)
    matrix[...] = along_z()
    for item in range(2):
        assemble(field, item, 2 + item, slab, own, other, near, far, swapped_near, swapped_far)
    misfit = jnp.sum(misfits[...], axis=0)
    spots = receivers[...]
    row = (spots >> 7) - (slab - 4) * (TX * AY)
    rows = lax.broadcasted_iota(jnp.int32, (PLANES * AY, NREC), 0)
    at_row[...] = jnp.where(rows == row, 1.0, 0.0).astype(jnp.bfloat16)
    at_lane = rows[0:TZ] == (spots & 127)
    image[...] = jnp.zeros((TX, AY, TZ), jnp.float32)
    for i in range(STEPS):
        n = STEPS - i
        prev, cur = i & 1, 1 - (i & 1)
        low, high = 4 + 4 * i, PLANES - 4 - 4 * i
        parts = [jnp.where(at_lane, part.astype(jnp.float32), 0.0).astype(jnp.bfloat16) for part in split2(misfit[n - 1 : n])]
        sent = jnp.concatenate(parts, axis=0)
        for p in range(low, high, 16):
            q = min(p + 16, high)
            product = lax.dot_general(
                at_row[p * AY : q * AY], sent, (((1,), (1,)), ((), ())), preferred_element_type=jnp.float32
            )
            injected[p:q] = halves(product).reshape(q - p, AY, TZ)
        z_pass(field, cur, matrix, low, high, zpart)

        def planes(b, _, prev=prev, cur=cur, low=low):
            p = low + 8 * b
            for h in range(2):
                y = PAD + 8 * h
                middle, acc = xy_block(field, cur, p, h, zpart)
                change = courant[pl.ds(p, 8), 8 * h : 8 * h + 8, :] * acc + injected[pl.ds(p, 8), 8 * h : 8 * h + 8, :]
                field[prev, pl.ds(p, 8), y : y + 8, :] = (middle + middle) - field[prev, pl.ds(p, 8), y : y + 8, :] + change
            return 0

        lax.fori_loop(0, (high - low) // 8, planes, 0)
        image[...] += field[prev, OWN : OWN + TX, PAD : PAD + AY, :] * curvature[n - 1]
    out[...] = jnp.zeros(out.shape, jnp.float32)
    for k in range(2):
        speed = vel[k]
        out[first_row + k] = 2.0 / (speed * speed * speed) * image[:, 8 * k : 8 * k + 8, :]


def in_vmem(count):
    return [pl.BlockSpec(memory_space=pltpu.VMEM)] * count


def in_smem(count):
    return [pl.BlockSpec(memory_space=pltpu.SMEM)] * count


def inner(
    velocity,
    aperture,
    source_cell,
    wavelet,
    observed,
    receivers,
    checkpoint,
    forward_previous,
    forward_current,
    adjoint_next,
    adjoint_current,
):
    def shift(cells, by):
        return lax.ppermute(cells, DOM, [(i, (i + by) % SLABS) for i in range(SLABS)])

    def partner(cells):
        return lax.ppermute(cells, DOM, [(i, i ^ 1) for i in range(SLABS)])

    def next_chip(cells):
        return lax.ppermute(cells, DOM, [(i, (i + (-2 if i % 2 else 2)) % SLABS) for i in range(SLABS)])

    own = jnp.concatenate([forward_previous, forward_current, adjoint_next, adjoint_current], axis=0)
    column = lax.all_to_all(
        jnp.broadcast_to(velocity[None], (4,) + velocity.shape), "yh", 0, 0, tiled=True
    )
    other = partner(own)
    rows = lax.all_to_all(jnp.broadcast_to(column[None], (4,) + column.shape), "x", 0, 0, tiled=True)
    near = next_chip(jnp.stack([own, other]))
    rows = rows.reshape((16,) + velocity.shape[1:])
    vel = lax.dynamic_slice_in_dim(rows, aperture[0, 0, 0] // SLABS, 2, 0)
    vel_left = shift(vel, 1)
    vel_right = shift(vel, -1)
    far = next_chip(near)
    vel_packed = jnp.stack([vel_left, vel, vel_right])
    vel_far_left = shift(vel_packed, 3)
    vel_far_right = shift(vel_packed, -3)
    swapped_near = partner(near)
    swapped_far = partner(far)
    fields = (own, other, near, far, swapped_near, swapped_far)

    slab_steps = (STEPS, TX, AY, TZ)
    region = (PLANES, AY, TZ)
    f32 = jnp.float32
    padded = pltpu.VMEM((2, PLANES, AY + 2 * PAD, TZ), f32)
    matrix = pltpu.VMEM((2 * TZ, 2 * TZ), jnp.bfloat16)
    limit = pltpu.CompilerParams(vmem_limit_bytes=32 << 20)
    curvature, misfit, courant = pl.pallas_call(
        forward_kernel,
        in_specs=in_smem(4) + in_vmem(13),
        out_specs=in_vmem(3),
        out_shape=[
            jax.ShapeDtypeStruct(slab_steps, f32),
            jax.ShapeDtypeStruct((SLABS, STEPS, NREC), f32),
            jax.ShapeDtypeStruct(region, f32),
        ],
        scratch_shapes=[
            padded,
            pltpu.VMEM(region, f32),
            pltpu.VMEM((STEPS, TX * AY, TZ), f32),
            pltpu.VMEM(region, f32),
            matrix,
        ],
        compiler_params=limit,
        name="forward",
    )(
        aperture, source_cell, checkpoint, wavelet, observed, receivers, *fields,
        vel, vel_left, vel_right, vel_far_left, vel_far_right,
    )

    misfits = lax.all_to_all(misfit[:, None], DOM, 0, 0, tiled=True).reshape(SLABS, STEPS, NREC)

    terms = pl.pallas_call(
        adjoint_kernel,
        in_specs=in_smem(1) + in_vmem(11),
        out_specs=in_vmem(1)[0],
        out_shape=jax.ShapeDtypeStruct((16, TX, 8, TZ), f32),
        scratch_shapes=[
            padded,
            pltpu.VMEM(region, f32),
            pltpu.VMEM((TX, AY, TZ), f32),
            pltpu.VMEM(region, f32),
            matrix,
            pltpu.VMEM((PLANES * AY, NREC), jnp.bfloat16),
        ],
        compiler_params=limit,
        name="adjoint",
    )(
        aperture, receivers, misfits, *fields,
        vel, courant, curvature,
    )
    landed = lax.all_to_all(terms, SHOT, 0, 0, tiled=True)
    return jnp.sum(landed, axis=0, keepdims=True)


def solution(mesh):
    split = Mesh(mesh.devices.reshape(4, 4, 2, 8, 2), SHOT + DOM)
    placed = (
        P(SHOT + DOM, None, None, None),
        P(SHOT, DOM, None),
        P(SHOT),
        P(SHOT, None),
        P(SHOT, None, None),
        P(SHOT, None),
        P(SHOT),
        P(SHOT, DOM, None, None),
        P(SHOT, DOM, None, None),
        P(SHOT, DOM, None, None),
        P(SHOT, DOM, None, None),
    )
    return jax.shard_map(
        inner,
        mesh=split,
        in_specs=placed,
        out_specs=P(SHOT + DOM, None, None, None),
        check_vma=False,
    )
```

```python
import jax
import jax.numpy as jnp
from jax import lax
from jax.experimental import pallas as pl
from jax.experimental.pallas import tpu as pltpu
from jax.sharding import Mesh, PartitionSpec as P


STEPS = 8
STENCIL_WEIGHTS = (-205.0 / 72.0, 8.0 / 5.0, -1.0 / 5.0, 8.0 / 315.0, -1.0 / 560.0)
STEP_SCALE = 0.088
DOM = ("yl", "z", "c")
SHOT = ("x", "yh")
SLABS = 32
TX, AY, TZ = 8, 16, 128
PLANES = 9 * TX
OWN = 4 * TX
PAD = 8
NREC = 256


def split2(x):
    high = x.astype(jnp.bfloat16)
    return high, (x - high.astype(jnp.float32)).astype(jnp.bfloat16)


def along_z():
    apart = jnp.abs(
        lax.broadcasted_iota(jnp.int32, (TZ, TZ), 0) - lax.broadcasted_iota(jnp.int32, (TZ, TZ), 1)
    )
    band = jnp.where(apart == 0, 3.0 * STENCIL_WEIGHTS[0], 0.0)
    for s in range(1, 5):
        band = jnp.where(apart == s, STENCIL_WEIGHTS[s], band)
    high, low = split2(band)
    top = jnp.concatenate([high, low], axis=1)
    return jnp.concatenate([top, jnp.concatenate([high, jnp.zeros_like(low)], axis=1)], axis=0)


def stack_parts(x):
    return jnp.concatenate(split2(x), axis=1)


def halves(product):
    return product[:, :TZ] + product[:, TZ:]


def z_pass(field, cur, matrix, low, high, zpart):
    for p in range(low, high, 16):
        q = min(p + 16, high)
        rows = field[cur, p:q, PAD : PAD + AY, :].reshape((q - p) * AY, TZ)
        product = jnp.dot(stack_parts(rows), matrix[...], preferred_element_type=jnp.float32)
        zpart[p:q] = halves(product).reshape(q - p, AY, TZ)


def xy_block(field, cur, p, h, zpart):
    y = PAD + 8 * h
    column = field[cur, pl.ds(p - 4, 16), y : y + 8, :]
    acc = zpart[pl.ds(p, 8), 8 * h : 8 * h + 8, :]
    for s in range(1, 5):
        near = column[4 + s : 12 + s] + column[4 - s : 12 - s]
        near = near + (field[cur, pl.ds(p, 8), y + s : y + 8 + s, :] + field[cur, pl.ds(p, 8), y - s : y + 8 - s, :])
        acc = acc + STENCIL_WEIGHTS[s] * near
    return column[4:12], acc


def assemble(field, which, item, slab, own, other, near, far, swapped_near, swapped_far):
    def put(j, value):
        there = slab + j
        inside = (there >= 0) & (there < SLABS)
        field[which, TX * (j + 4) : TX * (j + 5), PAD : PAD + AY, :] = jnp.where(inside, value, 0.0)

    put(0, own[item])

    @pl.when((slab & 1) == 0)
    def _():
        put(-4, far[0, item])
        put(-3, far[1, item])
        put(-2, near[0, item])
        put(-1, near[1, item])
        put(1, other[item])
        put(2, swapped_near[1, item])
        put(3, swapped_near[0, item])
        put(4, swapped_far[1, item])

    @pl.when((slab & 1) == 1)
    def _():
        put(-4, swapped_far[1, item])
        put(-3, swapped_near[0, item])
        put(-2, swapped_near[1, item])
        put(-1, other[item])
        put(1, near[1, item])
        put(2, near[0, item])
        put(3, far[1, item])
        put(4, far[0, item])


def clear_pads(field):
    zero = jnp.zeros((PLANES, PAD, TZ), jnp.float32)
    for b in range(2):
        field[b, :, 0:PAD, :] = zero
        field[b, :, PAD + AY : PAD + AY + PAD, :] = zero


def forward_kernel(
    aperture, source, checkpoint, wavelet, observed, receivers,
    own, other, near, far, swapped_near, swapped_far,
    vel, vel_left, vel_right, vel_far_left, vel_far_right,
    curvature, misfit, courant,
    field, update, samples, zpart, matrix,
):
    slab = aperture[0, 0, 0] & (SLABS - 1)
    clear_pads(field)
    matrix[...] = along_z()
    for item in range(2):
        assemble(field, item, item, slab, own, other, near, far, swapped_near, swapped_far)
    tiles = (
        [(vel_far_left, k) for k in range(3)] + [(vel_left, None), (vel, None), (vel_right, None)] + [(vel_far_right, k) for k in range(3)]
    )
    for j in range(9):
        there = slab + (j - 4)
        inside = (there >= 0) & (there < SLABS)
        ref, k = tiles[j]
        for row in range(2):
            speed = ref[row] if k is None else ref[k, row]
            speed = jnp.where(inside, STEP_SCALE * speed, 0.0)
            courant[TX * j : TX * (j + 1), 8 * row : 8 * row + 8, :] = speed * speed

    lane = lax.broadcasted_iota(jnp.int32, (AY, TZ), 1)
    suby = lax.broadcasted_iota(jnp.int32, (AY, TZ), 0)
    cell = source[0]
    source_x = (cell >> 11) - (slab - 4) * TX
    source_here = (source_x >= 0) & (source_x < PLANES)
    source_own = (source_x >= OWN) & (source_x < OWN + TX)
    spot = (suby == ((cell >> 7) & 15)) & (lane == (cell & 127))
    start = checkpoint[0]

    for n in range(STEPS):
        prev, cur = n & 1, 1 - (n & 1)
        low, high = 4 + 4 * n, PLANES - 4 - 4 * n
        z_pass(field, cur, matrix, low, high, zpart)

        def planes(b, _, prev=prev, cur=cur, low=low):
            p = low + 8 * b
            for h in range(2):
                y = PAD + 8 * h
                middle, acc = xy_block(field, cur, p, h, zpart)
                change = courant[pl.ds(p, 8), 8 * h : 8 * h + 8, :] * acc
                update[pl.ds(p, 8), 8 * h : 8 * h + 8, :] = change
                field[prev, pl.ds(p, 8), y : y + 8, :] = (middle + middle) - field[prev, pl.ds(p, 8), y : y + 8, :] + change
            return 0

        lax.fori_loop(0, (high - low) // 8, planes, 0)
        pulse = jnp.where(spot, wavelet[0, start + n], 0.0)

        @pl.when(source_here)
        def _(prev=prev, pulse=pulse):
            field[prev, source_x, PAD : PAD + AY, :] = field[prev, source_x, PAD : PAD + AY, :] + pulse

        @pl.when(source_own)
        def _(pulse=pulse):
            update[source_x] = update[source_x] + pulse

        curvature[n] = update[OWN : OWN + TX]
        samples[n] = field[prev, OWN : OWN + TX, PAD : PAD + AY, :].reshape(TX * AY, TZ)

    spots = receivers[...]
    row = (spots >> 7) - slab * (TX * AY)
    rows = lax.broadcasted_iota(jnp.int32, (TX * AY, NREC), 0)
    at_row = jnp.where(rows == row, 1.0, 0.0)
    at_lane = jnp.where(rows == (spots & 127), 1.0, 0.0).astype(jnp.bfloat16)
    at_lane = jnp.concatenate([at_lane, at_lane], axis=0)
    here = (row >= 0) & (row < TX * AY)
    taken = []
    for n in range(STEPS):
        product = jnp.dot(stack_parts(samples[n]), at_lane, preferred_element_type=jnp.float32)
        recorded = observed[0, pl.ds(start + n, 1), :]
        taken.append(jnp.sum(product * at_row, axis=0, keepdims=True) - jnp.where(here, recorded, 0.0))
    found = jnp.concatenate(taken, axis=0)
    for k in range(SLABS):
        misfit[k] = found


def adjoint_kernel(
    aperture, receivers, misfits,
    own, other, near, far, swapped_near, swapped_far,
    vel, courant, curvature,
    out,
    field, injected, image, zpart, matrix, at_row,
):
    slab = aperture[0, 0, 0] & (SLABS - 1)
    first_row = aperture[0, 0, 0] >> 5
    clear_pads(field)
    matrix[...] = along_z()
    for item in range(2):
        assemble(field, item, 2 + item, slab, own, other, near, far, swapped_near, swapped_far)
    misfit = jnp.sum(misfits[...], axis=0)
    spots = receivers[...]
    row = (spots >> 7) - (slab - 4) * (TX * AY)
    rows = lax.broadcasted_iota(jnp.int32, (PLANES * AY, NREC), 0)
    at_row[...] = jnp.where(rows == row, 1.0, 0.0).astype(jnp.bfloat16)
    at_lane = rows[0:TZ] == (spots & 127)
    image[...] = jnp.zeros((TX, AY, TZ), jnp.float32)
    for i in range(STEPS):
        n = STEPS - i
        prev, cur = i & 1, 1 - (i & 1)
        low, high = 4 + 4 * i, PLANES - 4 - 4 * i
        parts = [jnp.where(at_lane, part.astype(jnp.float32), 0.0).astype(jnp.bfloat16) for part in split2(misfit[n - 1 : n])]
        sent = jnp.concatenate(parts, axis=0)
        for p in range(low, high, 16):
            q = min(p + 16, high)
            product = lax.dot_general(
                at_row[p * AY : q * AY], sent, (((1,), (1,)), ((), ())), preferred_element_type=jnp.float32
            )
            injected[p:q] = halves(product).reshape(q - p, AY, TZ)
        z_pass(field, cur, matrix, low, high, zpart)

        def planes(b, _, prev=prev, cur=cur, low=low):
            p = low + 8 * b
            for h in range(2):
                y = PAD + 8 * h
                middle, acc = xy_block(field, cur, p, h, zpart)
                change = courant[pl.ds(p, 8), 8 * h : 8 * h + 8, :] * acc + injected[pl.ds(p, 8), 8 * h : 8 * h + 8, :]
                field[prev, pl.ds(p, 8), y : y + 8, :] = (middle + middle) - field[prev, pl.ds(p, 8), y : y + 8, :] + change
            return 0

        lax.fori_loop(0, (high - low) // 8, planes, 0)
        image[...] += field[prev, OWN : OWN + TX, PAD : PAD + AY, :] * curvature[n - 1]
    out[...] = jnp.zeros(out.shape, jnp.float32)
    for k in range(2):
        speed = vel[k]
        out[first_row + k] = 2.0 / (speed * speed * speed) * image[:, 8 * k : 8 * k + 8, :]


def pack_kernel(a, b, c, d, out, sems):
    copies = [pltpu.make_async_copy(ref.at[0], out.at[k], sems.at[k]) for k, ref in enumerate((a, b, c, d))]
    for copy in copies:
        copy.start()
    for copy in copies:
        copy.wait()


def pack(*fields):
    return pl.pallas_call(
        pack_kernel,
        in_specs=[pl.BlockSpec(memory_space=pltpu.HBM)] * 4,
        out_specs=pl.BlockSpec(memory_space=pltpu.VMEM),
        out_shape=jax.ShapeDtypeStruct((4,) + fields[0].shape[1:], jnp.float32),
        scratch_shapes=[pltpu.SemaphoreType.DMA((4,))],
        name="pack",
    )(*fields)


def in_vmem(count):
    return [pl.BlockSpec(memory_space=pltpu.VMEM)] * count


def in_smem(count):
    return [pl.BlockSpec(memory_space=pltpu.SMEM)] * count


def inner(
    velocity,
    aperture,
    source_cell,
    wavelet,
    observed,
    receivers,
    checkpoint,
    forward_previous,
    forward_current,
    adjoint_next,
    adjoint_current,
):
    def shift(cells, by):
        return lax.ppermute(cells, DOM, [(i, (i + by) % SLABS) for i in range(SLABS)])

    def partner(cells):
        return lax.ppermute(cells, DOM, [(i, i ^ 1) for i in range(SLABS)])

    def next_chip(cells):
        return lax.ppermute(cells, DOM, [(i, (i + (-2 if i % 2 else 2)) % SLABS) for i in range(SLABS)])

    own = pack(forward_previous, forward_current, adjoint_next, adjoint_current)
    column = lax.all_to_all(
        jnp.broadcast_to(velocity[None], (4,) + velocity.shape), "yh", 0, 0, tiled=True
    )
    other = partner(own)
    rows = lax.all_to_all(jnp.broadcast_to(column[None], (4,) + column.shape), "x", 0, 0, tiled=True)
    near = next_chip(jnp.stack([own, other]))
    rows = rows.reshape((16,) + velocity.shape[1:])
    vel = lax.dynamic_slice_in_dim(rows, aperture[0, 0, 0] // SLABS, 2, 0)
    vel_left = shift(vel, 1)
    vel_right = shift(vel, -1)
    far = next_chip(near)
    vel_packed = jnp.stack([vel_left, vel, vel_right])
    vel_far_left = shift(vel_packed, 3)
    vel_far_right = shift(vel_packed, -3)
    swapped_near = partner(near)
    swapped_far = partner(far)
    fields = (own, other, near, far, swapped_near, swapped_far)

    slab_steps = (STEPS, TX, AY, TZ)
    region = (PLANES, AY, TZ)
    f32 = jnp.float32
    padded = pltpu.VMEM((2, PLANES, AY + 2 * PAD, TZ), f32)
    matrix = pltpu.VMEM((2 * TZ, 2 * TZ), jnp.bfloat16)
    limit = pltpu.CompilerParams(vmem_limit_bytes=16 << 20)
    curvature, misfit, courant = pl.pallas_call(
        forward_kernel,
        in_specs=in_smem(4) + in_vmem(13),
        out_specs=in_vmem(3),
        out_shape=[
            jax.ShapeDtypeStruct(slab_steps, f32),
            jax.ShapeDtypeStruct((SLABS, STEPS, NREC), f32),
            jax.ShapeDtypeStruct(region, f32),
        ],
        scratch_shapes=[
            padded,
            pltpu.VMEM(region, f32),
            pltpu.VMEM((STEPS, TX * AY, TZ), f32),
            pltpu.VMEM(region, f32),
            matrix,
        ],
        compiler_params=limit,
        name="forward",
    )(
        aperture, source_cell, checkpoint, wavelet, observed, receivers, *fields,
        vel, vel_left, vel_right, vel_far_left, vel_far_right,
    )

    misfits = lax.all_to_all(misfit[:, None], DOM, 0, 0, tiled=True).reshape(SLABS, STEPS, NREC)

    terms = pl.pallas_call(
        adjoint_kernel,
        in_specs=in_smem(1) + in_vmem(11),
        out_specs=in_vmem(1)[0],
        out_shape=jax.ShapeDtypeStruct((16, TX, 8, TZ), f32),
        scratch_shapes=[
            padded,
            pltpu.VMEM(region, f32),
            pltpu.VMEM((TX, AY, TZ), f32),
            pltpu.VMEM(region, f32),
            matrix,
            pltpu.VMEM((PLANES * AY, NREC), jnp.bfloat16),
        ],
        compiler_params=limit,
        name="adjoint",
    )(
        aperture, receivers, misfits, *fields,
        vel, courant, curvature,
    )
    landed = lax.all_to_all(terms, SHOT, 0, 0, tiled=True)
    return jnp.sum(landed, axis=0, keepdims=True)


def solution(mesh):
    split = Mesh(mesh.devices.reshape(4, 4, 2, 8, 2), SHOT + DOM)
    placed = (
        P(SHOT + DOM, None, None, None),
        P(SHOT, DOM, None),
        P(SHOT),
        P(SHOT, None),
        P(SHOT, None, None),
        P(SHOT, None),
        P(SHOT),
        P(SHOT, DOM, None, None),
        P(SHOT, DOM, None, None),
        P(SHOT, DOM, None, None),
        P(SHOT, DOM, None, None),
    )
    return jax.shard_map(
        inner,
        mesh=split,
        in_specs=placed,
        out_specs=P(SHOT + DOM, None, None, None),
        check_vma=False,
    )
```

```python
import jax
import jax.numpy as jnp
from jax import lax
from jax.experimental import pallas as pl
from jax.experimental.pallas import tpu as pltpu
from jax.sharding import Mesh, PartitionSpec as P


STEPS = 8
STENCIL_WEIGHTS = (-205.0 / 72.0, 8.0 / 5.0, -1.0 / 5.0, 8.0 / 315.0, -1.0 / 560.0)
STEP_SCALE = 0.088
DOM = ("yl", "z", "c")
SHOT = ("x", "yh")
SLABS = 32
TX, AY, TZ = 8, 16, 128
PLANES = 9 * TX
OWN = 4 * TX
PAD = 8
NREC = 256


def split2(x):
    high = x.astype(jnp.bfloat16)
    return high, (x - high.astype(jnp.float32)).astype(jnp.bfloat16)


def along_z():
    apart = jnp.abs(
        lax.broadcasted_iota(jnp.int32, (TZ, TZ), 0) - lax.broadcasted_iota(jnp.int32, (TZ, TZ), 1)
    )
    band = jnp.where(apart == 0, 3.0 * STENCIL_WEIGHTS[0], 0.0)
    for s in range(1, 5):
        band = jnp.where(apart == s, STENCIL_WEIGHTS[s], band)
    high, low = split2(band)
    top = jnp.concatenate([high, low], axis=1)
    return jnp.concatenate([top, jnp.concatenate([high, jnp.zeros_like(low)], axis=1)], axis=0)


def stack_parts(x):
    return jnp.concatenate(split2(x), axis=1)


def halves(product):
    return product[:, :TZ] + product[:, TZ:]


def z_pass(field, cur, matrix, low, high, zpart):
    for p in range(low, high, 16):
        q = min(p + 16, high)
        rows = field[cur, p:q, PAD : PAD + AY, :].reshape((q - p) * AY, TZ)
        product = jnp.dot(stack_parts(rows), matrix[...], preferred_element_type=jnp.float32)
        zpart[p:q] = halves(product).reshape(q - p, AY, TZ)


def xy_block(field, cur, p, h, zpart):
    y = PAD + 8 * h
    column = field[cur, pl.ds(p - 4, 16), y : y + 8, :]
    acc = zpart[pl.ds(p, 8), 8 * h : 8 * h + 8, :]
    for s in range(1, 5):
        near = column[4 + s : 12 + s] + column[4 - s : 12 - s]
        near = near + (field[cur, pl.ds(p, 8), y + s : y + 8 + s, :] + field[cur, pl.ds(p, 8), y - s : y + 8 - s, :])
        acc = acc + STENCIL_WEIGHTS[s] * near
    return column[4:12], acc


def assemble(field, which, item, slab, own, other, near, far, swapped_near, swapped_far):
    def put(j, value):
        there = slab + j
        inside = (there >= 0) & (there < SLABS)
        field[which, TX * (j + 4) : TX * (j + 5), PAD : PAD + AY, :] = jnp.where(inside, value, 0.0)

    put(0, own[item])

    @pl.when((slab & 1) == 0)
    def _():
        put(-4, far[0, item])
        put(-3, far[1, item])
        put(-2, near[0, item])
        put(-1, near[1, item])
        put(1, other[item])
        put(2, swapped_near[1, item])
        put(3, swapped_near[0, item])
        put(4, swapped_far[1, item])

    @pl.when((slab & 1) == 1)
    def _():
        put(-4, swapped_far[1, item])
        put(-3, swapped_near[0, item])
        put(-2, swapped_near[1, item])
        put(-1, other[item])
        put(1, near[1, item])
        put(2, near[0, item])
        put(3, far[1, item])
        put(4, far[0, item])


def clear_pads(field):
    zero = jnp.zeros((PLANES, PAD, TZ), jnp.float32)
    for b in range(2):
        field[b, :, 0:PAD, :] = zero
        field[b, :, PAD + AY : PAD + AY + PAD, :] = zero


def forward_kernel(
    aperture, source, checkpoint, wavelet, observed, receivers,
    own, other, near, far, swapped_near, swapped_far,
    vel, vel_left, vel_right, vel_far_left, vel_far_right,
    curvature, misfit, courant,
    field, update, samples, zpart, matrix,
):
    slab = aperture[0, 0, 0] & (SLABS - 1)
    clear_pads(field)
    matrix[...] = along_z()
    for item in range(2):
        assemble(field, item, item, slab, own, other, near, far, swapped_near, swapped_far)
    tiles = (
        [(vel_far_left, k) for k in range(3)] + [(vel_left, None), (vel, None), (vel_right, None)] + [(vel_far_right, k) for k in range(3)]
    )
    for j in range(9):
        there = slab + (j - 4)
        inside = (there >= 0) & (there < SLABS)
        ref, k = tiles[j]
        for row in range(2):
            speed = ref[row] if k is None else ref[k, row]
            speed = jnp.where(inside, STEP_SCALE * speed, 0.0)
            courant[TX * j : TX * (j + 1), 8 * row : 8 * row + 8, :] = speed * speed

    lane = lax.broadcasted_iota(jnp.int32, (AY, TZ), 1)
    suby = lax.broadcasted_iota(jnp.int32, (AY, TZ), 0)
    cell = source[0]
    source_x = (cell >> 11) - (slab - 4) * TX
    source_here = (source_x >= 0) & (source_x < PLANES)
    source_own = (source_x >= OWN) & (source_x < OWN + TX)
    spot = (suby == ((cell >> 7) & 15)) & (lane == (cell & 127))
    start = checkpoint[0]

    for n in range(STEPS):
        prev, cur = n & 1, 1 - (n & 1)
        low, high = 4 + 4 * n, PLANES - 4 - 4 * n
        z_pass(field, cur, matrix, low, high, zpart)

        def planes(b, _, prev=prev, cur=cur, low=low):
            p = low + 8 * b
            for h in range(2):
                y = PAD + 8 * h
                middle, acc = xy_block(field, cur, p, h, zpart)
                change = courant[pl.ds(p, 8), 8 * h : 8 * h + 8, :] * acc
                update[pl.ds(p, 8), 8 * h : 8 * h + 8, :] = change
                field[prev, pl.ds(p, 8), y : y + 8, :] = (middle + middle) - field[prev, pl.ds(p, 8), y : y + 8, :] + change
            return 0

        lax.fori_loop(0, (high - low) // 8, planes, 0)
        pulse = jnp.where(spot, wavelet[0, start + n], 0.0)

        @pl.when(source_here)
        def _(prev=prev, pulse=pulse):
            field[prev, source_x, PAD : PAD + AY, :] = field[prev, source_x, PAD : PAD + AY, :] + pulse

        @pl.when(source_own)
        def _(pulse=pulse):
            update[source_x] = update[source_x] + pulse

        curvature[n] = update[OWN : OWN + TX]
        samples[n] = field[prev, OWN : OWN + TX, PAD : PAD + AY, :].reshape(TX * AY, TZ)

    spots = receivers[...]
    row = (spots >> 7) - slab * (TX * AY)
    rows = lax.broadcasted_iota(jnp.int32, (TX * AY, NREC), 0)
    at_row = jnp.where(rows == row, 1.0, 0.0)
    at_lane = jnp.where(rows == (spots & 127), 1.0, 0.0).astype(jnp.bfloat16)
    at_lane = jnp.concatenate([at_lane, at_lane], axis=0)
    here = (row >= 0) & (row < TX * AY)
    taken = []
    for n in range(STEPS):
        product = jnp.dot(stack_parts(samples[n]), at_lane, preferred_element_type=jnp.float32)
        recorded = observed[0, pl.ds(start + n, 1), :]
        taken.append(jnp.sum(product * at_row, axis=0, keepdims=True) - jnp.where(here, recorded, 0.0))
    found = jnp.concatenate(taken, axis=0)
    for k in range(SLABS):
        misfit[k] = found


def adjoint_kernel(
    aperture, receivers, misfits,
    own, other, near, far, swapped_near, swapped_far,
    vel, courant, curvature,
    out,
    field, injected, image, zpart, matrix, at_row,
):
    slab = aperture[0, 0, 0] & (SLABS - 1)
    first_row = aperture[0, 0, 0] >> 5
    clear_pads(field)
    matrix[...] = along_z()
    for item in range(2):
        assemble(field, item, 2 + item, slab, own, other, near, far, swapped_near, swapped_far)
    misfit = jnp.sum(misfits[...], axis=0)
    spots = receivers[...]
    row = (spots >> 7) - (slab - 4) * (TX * AY)
    rows = lax.broadcasted_iota(jnp.int32, (PLANES * AY, NREC), 0)
    at_row[...] = jnp.where(rows == row, 1.0, 0.0).astype(jnp.bfloat16)
    at_lane = rows[0:TZ] == (spots & 127)
    image[...] = jnp.zeros((TX, AY, TZ), jnp.float32)
    for i in range(STEPS):
        n = STEPS - i
        prev, cur = i & 1, 1 - (i & 1)
        low, high = 4 + 4 * i, PLANES - 4 - 4 * i
        parts = [jnp.where(at_lane, part.astype(jnp.float32), 0.0).astype(jnp.bfloat16) for part in split2(misfit[n - 1 : n])]
        sent = jnp.concatenate(parts, axis=0)
        for p in range(low, high, 16):
            q = min(p + 16, high)
            product = lax.dot_general(
                at_row[p * AY : q * AY], sent, (((1,), (1,)), ((), ())), preferred_element_type=jnp.float32
            )
            injected[p:q] = halves(product).reshape(q - p, AY, TZ)
        z_pass(field, cur, matrix, low, high, zpart)

        def planes(b, _, prev=prev, cur=cur, low=low):
            p = low + 8 * b
            for h in range(2):
                y = PAD + 8 * h
                middle, acc = xy_block(field, cur, p, h, zpart)
                change = courant[pl.ds(p, 8), 8 * h : 8 * h + 8, :] * acc + injected[pl.ds(p, 8), 8 * h : 8 * h + 8, :]
                field[prev, pl.ds(p, 8), y : y + 8, :] = (middle + middle) - field[prev, pl.ds(p, 8), y : y + 8, :] + change
            return 0

        lax.fori_loop(0, (high - low) // 8, planes, 0)
        image[...] += field[prev, OWN : OWN + TX, PAD : PAD + AY, :] * curvature[n - 1]
    out[...] = jnp.zeros(out.shape, jnp.float32)
    for k in range(2):
        speed = vel[k]
        target = first_row + k
        out[target & 3, 0:TX] = 2.0 / (speed * speed * speed) * image[:, 8 * k : 8 * k + 8, :]
        out[target & 3, TX] = jnp.full((8, TZ), target >> 2, jnp.int32).astype(jnp.float32)


def pack_kernel(a, b, c, d, out, sems):
    copies = [pltpu.make_async_copy(ref.at[0], out.at[k], sems.at[k]) for k, ref in enumerate((a, b, c, d))]
    for copy in copies:
        copy.start()
    for copy in copies:
        copy.wait()


def pack(*fields):
    return pl.pallas_call(
        pack_kernel,
        in_specs=[pl.BlockSpec(memory_space=pltpu.HBM)] * 4,
        out_specs=pl.BlockSpec(memory_space=pltpu.VMEM),
        out_shape=jax.ShapeDtypeStruct((4,) + fields[0].shape[1:], jnp.float32),
        scratch_shapes=[pltpu.SemaphoreType.DMA((4,))],
        name="pack",
    )(*fields)


def in_vmem(count):
    return [pl.BlockSpec(memory_space=pltpu.VMEM)] * count


def in_smem(count):
    return [pl.BlockSpec(memory_space=pltpu.SMEM)] * count


def inner(
    velocity,
    aperture,
    source_cell,
    wavelet,
    observed,
    receivers,
    checkpoint,
    forward_previous,
    forward_current,
    adjoint_next,
    adjoint_current,
):
    def shift(cells, by):
        return lax.ppermute(cells, DOM, [(i, (i + by) % SLABS) for i in range(SLABS)])

    def partner(cells):
        return lax.ppermute(cells, DOM, [(i, i ^ 1) for i in range(SLABS)])

    def next_chip(cells):
        return lax.ppermute(cells, DOM, [(i, (i + (-2 if i % 2 else 2)) % SLABS) for i in range(SLABS)])

    own = pack(forward_previous, forward_current, adjoint_next, adjoint_current)
    column = lax.all_to_all(
        jnp.broadcast_to(velocity[None], (4,) + velocity.shape), "yh", 0, 0, tiled=True
    )
    other = partner(own)
    rows = lax.all_to_all(jnp.broadcast_to(column[None], (4,) + column.shape), "x", 0, 0, tiled=True)
    near = next_chip(jnp.stack([own, other]))
    rows = rows.reshape((16,) + velocity.shape[1:])
    vel = lax.dynamic_slice_in_dim(rows, aperture[0, 0, 0] // SLABS, 2, 0)
    vel_left = shift(vel, 1)
    vel_right = shift(vel, -1)
    far = next_chip(near)
    vel_packed = jnp.stack([vel_left, vel, vel_right])
    vel_far_left = shift(vel_packed, 3)
    vel_far_right = shift(vel_packed, -3)
    swapped_near = partner(near)
    swapped_far = partner(far)
    fields = (own, other, near, far, swapped_near, swapped_far)

    slab_steps = (STEPS, TX, AY, TZ)
    region = (PLANES, AY, TZ)
    f32 = jnp.float32
    padded = pltpu.VMEM((2, PLANES, AY + 2 * PAD, TZ), f32)
    matrix = pltpu.VMEM((2 * TZ, 2 * TZ), jnp.bfloat16)
    limit = pltpu.CompilerParams(vmem_limit_bytes=16 << 20)
    curvature, misfit, courant = pl.pallas_call(
        forward_kernel,
        in_specs=in_smem(4) + in_vmem(13),
        out_specs=in_vmem(3),
        out_shape=[
            jax.ShapeDtypeStruct(slab_steps, f32),
            jax.ShapeDtypeStruct((SLABS, STEPS, NREC), f32),
            jax.ShapeDtypeStruct(region, f32),
        ],
        scratch_shapes=[
            padded,
            pltpu.VMEM(region, f32),
            pltpu.VMEM((STEPS, TX * AY, TZ), f32),
            pltpu.VMEM(region, f32),
            matrix,
        ],
        compiler_params=limit,
        name="forward",
    )(
        aperture, source_cell, checkpoint, wavelet, observed, receivers, *fields,
        vel, vel_left, vel_right, vel_far_left, vel_far_right,
    )

    misfits = lax.all_to_all(misfit[:, None], DOM, 0, 0, tiled=True).reshape(SLABS, STEPS, NREC)

    terms = pl.pallas_call(
        adjoint_kernel,
        in_specs=in_smem(1) + in_vmem(11),
        out_specs=in_vmem(1)[0],
        out_shape=jax.ShapeDtypeStruct((4, TX + 1, 8, TZ), f32),
        scratch_shapes=[
            padded,
            pltpu.VMEM(region, f32),
            pltpu.VMEM((TX, AY, TZ), f32),
            pltpu.VMEM(region, f32),
            matrix,
            pltpu.VMEM((PLANES * AY, NREC), jnp.bfloat16),
        ],
        compiler_params=limit,
        name="adjoint",
    )(
        aperture, receivers, misfits, *fields,
        vel, courant, curvature,
    )
    landed = lax.all_to_all(terms, "yh", 0, 0, tiled=True)
    tags = jnp.arange(4, dtype=jnp.float32).reshape(4, 1, 1, 1, 1)
    sums = jnp.sum(jnp.where(landed[None, :, TX:] == tags, landed[None, :, 0:TX], 0.0), axis=1)
    landed = lax.all_to_all(sums, "x", 0, 0, tiled=True)
    return jnp.sum(landed, axis=0, keepdims=True)


def solution(mesh):
    split = Mesh(mesh.devices.reshape(4, 4, 2, 8, 2), SHOT + DOM)
    placed = (
        P(SHOT + DOM, None, None, None),
        P(SHOT, DOM, None),
        P(SHOT),
        P(SHOT, None),
        P(SHOT, None, None),
        P(SHOT, None),
        P(SHOT),
        P(SHOT, DOM, None, None),
        P(SHOT, DOM, None, None),
        P(SHOT, DOM, None, None),
        P(SHOT, DOM, None, None),
    )
    return jax.shard_map(
        inner,
        mesh=split,
        in_specs=placed,
        out_specs=P(SHOT + DOM, None, None, None),
        check_vma=False,
    )
```

```python
import jax
import jax.numpy as jnp
from jax import lax
from jax.experimental import pallas as pl
from jax.experimental.pallas import tpu as pltpu
from jax.sharding import Mesh, PartitionSpec as P


STEPS = 8
STENCIL_WEIGHTS = (-205.0 / 72.0, 8.0 / 5.0, -1.0 / 5.0, 8.0 / 315.0, -1.0 / 560.0)
STEP_SCALE = 0.088
DOM = ("yl", "z", "c")
SHOT = ("x", "yh")
SLABS = 32
TX, AY, TZ = 8, 16, 128
PLANES = 9 * TX
OWN = 4 * TX
PAD = 8
NREC = 256


def split2(x):
    high = x.astype(jnp.bfloat16)
    return high, (x - high.astype(jnp.float32)).astype(jnp.bfloat16)


def along_z():
    apart = jnp.abs(
        lax.broadcasted_iota(jnp.int32, (TZ, TZ), 0) - lax.broadcasted_iota(jnp.int32, (TZ, TZ), 1)
    )
    band = jnp.where(apart == 0, 3.0 * STENCIL_WEIGHTS[0], 0.0)
    for s in range(1, 5):
        band = jnp.where(apart == s, STENCIL_WEIGHTS[s], band)
    high, low = split2(band)
    top = jnp.concatenate([high, low], axis=1)
    return jnp.concatenate([top, jnp.concatenate([high, jnp.zeros_like(low)], axis=1)], axis=0)


def stack_parts(x):
    return jnp.concatenate(split2(x), axis=1)


def halves(product):
    return product[:, :TZ] + product[:, TZ:]


def z_pass(field, cur, matrix, low, high, zpart):
    for p in range(low, high, 16):
        q = min(p + 16, high)
        rows = field[cur, p:q, PAD : PAD + AY, :].reshape((q - p) * AY, TZ)
        product = jnp.dot(stack_parts(rows), matrix[...], preferred_element_type=jnp.float32)
        zpart[p:q] = halves(product).reshape(q - p, AY, TZ)


def xy_block(field, cur, p, h, zpart):
    y = PAD + 8 * h
    column = field[cur, pl.ds(p - 4, 16), y : y + 8, :]
    acc = zpart[pl.ds(p, 8), 8 * h : 8 * h + 8, :]
    for s in range(1, 5):
        near = column[4 + s : 12 + s] + column[4 - s : 12 - s]
        near = near + (field[cur, pl.ds(p, 8), y + s : y + 8 + s, :] + field[cur, pl.ds(p, 8), y - s : y + 8 - s, :])
        acc = acc + STENCIL_WEIGHTS[s] * near
    return column[4:12], acc


def assemble(field, which, item, slab, own, other, near, far, swapped_near, swapped_far):
    def put(j, value):
        there = slab + j
        inside = (there >= 0) & (there < SLABS)
        field[which, TX * (j + 4) : TX * (j + 5), PAD : PAD + AY, :] = jnp.where(inside, value, 0.0)

    put(0, own[item])

    @pl.when((slab & 1) == 0)
    def _():
        put(-4, far[0, item])
        put(-3, far[1, item])
        put(-2, near[0, item])
        put(-1, near[1, item])
        put(1, other[item])
        put(2, swapped_near[1, item])
        put(3, swapped_near[0, item])
        put(4, swapped_far[1, item])

    @pl.when((slab & 1) == 1)
    def _():
        put(-4, swapped_far[1, item])
        put(-3, swapped_near[0, item])
        put(-2, swapped_near[1, item])
        put(-1, other[item])
        put(1, near[1, item])
        put(2, near[0, item])
        put(3, far[1, item])
        put(4, far[0, item])


def clear_pads(field):
    zero = jnp.zeros((PLANES, PAD, TZ), jnp.float32)
    for b in range(2):
        field[b, :, 0:PAD, :] = zero
        field[b, :, PAD + AY : PAD + AY + PAD, :] = zero


def forward_kernel(
    aperture, source, checkpoint, wavelet, observed, receivers,
    own, other, near, far, swapped_near, swapped_far,
    vel, vel_left, vel_right, vel_far_left, vel_far_right,
    curvature, misfit, courant,
    field, update, samples, zpart, matrix,
):
    slab = aperture[0, 0, 0] & (SLABS - 1)
    clear_pads(field)
    matrix[...] = along_z()
    for item in range(2):
        assemble(field, item, item, slab, own, other, near, far, swapped_near, swapped_far)
    pieces = (
        (-4, 4, 4, vel_far_left, 0), (-3, 0, 8, vel_far_left, 4), (-2, 0, 8, vel_far_left, 12),
        (-1, 0, 8, vel_left, 0), (0, 0, 8, vel, 0), (1, 0, 8, vel_right, 0),
        (2, 0, 8, vel_far_right, 0), (3, 0, 8, vel_far_right, 8), (4, 0, 4, vel_far_right, 16),
    )
    for j, first, count, ref, begin in pieces:
        there = slab + j
        inside = (there >= 0) & (there < SLABS)
        plane = TX * (j + 4) + first
        for row in range(2):
            speed = jnp.where(inside, STEP_SCALE * ref[row, begin : begin + count], 0.0)
            courant[plane : plane + count, 8 * row : 8 * row + 8, :] = speed * speed

    lane = lax.broadcasted_iota(jnp.int32, (AY, TZ), 1)
    suby = lax.broadcasted_iota(jnp.int32, (AY, TZ), 0)
    cell = source[0]
    source_x = (cell >> 11) - (slab - 4) * TX
    source_here = (source_x >= 0) & (source_x < PLANES)
    source_own = (source_x >= OWN) & (source_x < OWN + TX)
    spot = (suby == ((cell >> 7) & 15)) & (lane == (cell & 127))
    start = checkpoint[0]

    for n in range(STEPS):
        prev, cur = n & 1, 1 - (n & 1)
        low, high = 4 + 4 * n, PLANES - 4 - 4 * n
        z_pass(field, cur, matrix, low, high, zpart)

        def planes(b, _, prev=prev, cur=cur, low=low):
            p = low + 8 * b
            for h in range(2):
                y = PAD + 8 * h
                middle, acc = xy_block(field, cur, p, h, zpart)
                change = courant[pl.ds(p, 8), 8 * h : 8 * h + 8, :] * acc
                update[pl.ds(p, 8), 8 * h : 8 * h + 8, :] = change
                field[prev, pl.ds(p, 8), y : y + 8, :] = (middle + middle) - field[prev, pl.ds(p, 8), y : y + 8, :] + change
            return 0

        lax.fori_loop(0, (high - low) // 8, planes, 0)
        pulse = jnp.where(spot, wavelet[0, start + n], 0.0)

        @pl.when(source_here)
        def _(prev=prev, pulse=pulse):
            field[prev, source_x, PAD : PAD + AY, :] = field[prev, source_x, PAD : PAD + AY, :] + pulse

        @pl.when(source_own)
        def _(pulse=pulse):
            update[source_x] = update[source_x] + pulse

        curvature[n] = update[OWN : OWN + TX]
        samples[n] = field[prev, OWN : OWN + TX, PAD : PAD + AY, :].reshape(TX * AY, TZ)

    spots = receivers[...]
    row = (spots >> 7) - slab * (TX * AY)
    rows = lax.broadcasted_iota(jnp.int32, (TX * AY, NREC), 0)
    at_row = jnp.where(rows == row, 1.0, 0.0)
    at_lane = jnp.where(rows == (spots & 127), 1.0, 0.0).astype(jnp.bfloat16)
    at_lane = jnp.concatenate([at_lane, at_lane], axis=0)
    here = (row >= 0) & (row < TX * AY)
    taken = []
    for n in range(STEPS):
        product = jnp.dot(stack_parts(samples[n]), at_lane, preferred_element_type=jnp.float32)
        recorded = observed[0, pl.ds(start + n, 1), :]
        taken.append(jnp.sum(product * at_row, axis=0, keepdims=True) - jnp.where(here, recorded, 0.0))
    found = jnp.concatenate(taken, axis=0)
    for k in range(SLABS):
        misfit[k] = found


def adjoint_kernel(
    aperture, receivers, misfits,
    own, other, near, far, swapped_near, swapped_far,
    vel, courant, curvature,
    out,
    field, injected, image, zpart, matrix, at_row,
):
    slab = aperture[0, 0, 0] & (SLABS - 1)
    first_row = aperture[0, 0, 0] >> 5
    clear_pads(field)
    matrix[...] = along_z()
    for item in range(2):
        assemble(field, item, 2 + item, slab, own, other, near, far, swapped_near, swapped_far)
    misfit = jnp.sum(misfits[...], axis=0)
    spots = receivers[...]
    row = (spots >> 7) - (slab - 4) * (TX * AY)
    rows = lax.broadcasted_iota(jnp.int32, (PLANES * AY, NREC), 0)
    at_row[...] = jnp.where(rows == row, 1.0, 0.0).astype(jnp.bfloat16)
    at_lane = rows[0:TZ] == (spots & 127)
    image[...] = jnp.zeros((TX, AY, TZ), jnp.float32)
    for i in range(STEPS):
        n = STEPS - i
        prev, cur = i & 1, 1 - (i & 1)
        low, high = 4 + 4 * i, PLANES - 4 - 4 * i
        parts = [jnp.where(at_lane, part.astype(jnp.float32), 0.0).astype(jnp.bfloat16) for part in split2(misfit[n - 1 : n])]
        sent = jnp.concatenate(parts, axis=0)
        for p in range(low, high, 16):
            q = min(p + 16, high)
            product = lax.dot_general(
                at_row[p * AY : q * AY], sent, (((1,), (1,)), ((), ())), preferred_element_type=jnp.float32
            )
            injected[p:q] = halves(product).reshape(q - p, AY, TZ)
        z_pass(field, cur, matrix, low, high, zpart)

        def planes(b, _, prev=prev, cur=cur, low=low):
            p = low + 8 * b
            for h in range(2):
                y = PAD + 8 * h
                middle, acc = xy_block(field, cur, p, h, zpart)
                change = courant[pl.ds(p, 8), 8 * h : 8 * h + 8, :] * acc + injected[pl.ds(p, 8), 8 * h : 8 * h + 8, :]
                field[prev, pl.ds(p, 8), y : y + 8, :] = (middle + middle) - field[prev, pl.ds(p, 8), y : y + 8, :] + change
            return 0

        lax.fori_loop(0, (high - low) // 8, planes, 0)
        image[...] += field[prev, OWN : OWN + TX, PAD : PAD + AY, :] * curvature[n - 1]
    out[...] = jnp.zeros(out.shape, jnp.float32)
    for k in range(2):
        speed = vel[k]
        target = first_row + k
        out[target & 3, 0:TX] = 2.0 / (speed * speed * speed) * image[:, 8 * k : 8 * k + 8, :]
        out[target & 3, TX] = jnp.full((8, TZ), target >> 2, jnp.int32).astype(jnp.float32)


def pack_kernel(a, b, c, d, out, sems):
    copies = [pltpu.make_async_copy(ref.at[0], out.at[k], sems.at[k]) for k, ref in enumerate((a, b, c, d))]
    for copy in copies:
        copy.start()
    for copy in copies:
        copy.wait()


def pack(*fields):
    return pl.pallas_call(
        pack_kernel,
        in_specs=[pl.BlockSpec(memory_space=pltpu.HBM)] * 4,
        out_specs=pl.BlockSpec(memory_space=pltpu.VMEM),
        out_shape=jax.ShapeDtypeStruct((4,) + fields[0].shape[1:], jnp.float32),
        scratch_shapes=[pltpu.SemaphoreType.DMA((4,))],
        name="pack",
    )(*fields)


def in_vmem(count):
    return [pl.BlockSpec(memory_space=pltpu.VMEM)] * count


def in_smem(count):
    return [pl.BlockSpec(memory_space=pltpu.SMEM)] * count


def inner(
    velocity,
    aperture,
    source_cell,
    wavelet,
    observed,
    receivers,
    checkpoint,
    forward_previous,
    forward_current,
    adjoint_next,
    adjoint_current,
):
    def shift(cells, by):
        return lax.ppermute(cells, DOM, [(i, (i + by) % SLABS) for i in range(SLABS)])

    def partner(cells):
        return lax.ppermute(cells, DOM, [(i, i ^ 1) for i in range(SLABS)])

    def next_chip(cells):
        return lax.ppermute(cells, DOM, [(i, (i + (-2 if i % 2 else 2)) % SLABS) for i in range(SLABS)])

    own = pack(forward_previous, forward_current, adjoint_next, adjoint_current)
    column = lax.all_to_all(
        jnp.broadcast_to(velocity[None], (4,) + velocity.shape), "yh", 0, 0, tiled=True
    )
    other = partner(own)
    rows = lax.all_to_all(jnp.broadcast_to(column[None], (4,) + column.shape), "x", 0, 0, tiled=True)
    near = next_chip(jnp.stack([own, other]))
    rows = rows.reshape((16,) + velocity.shape[1:])
    vel = lax.dynamic_slice_in_dim(rows, aperture[0, 0, 0] // SLABS, 2, 0)
    vel_left = shift(vel, 1)
    vel_right = shift(vel, -1)
    far = next_chip(near)
    rightward = jnp.concatenate([vel_left[:, 4:], vel, vel_right], axis=1)
    leftward = jnp.concatenate([vel_left, vel, vel_right[:, :4]], axis=1)
    vel_far_left = shift(rightward, 3)
    vel_far_right = shift(leftward, -3)
    swapped_near = partner(near)
    swapped_far = partner(far)
    fields = (own, other, near, far, swapped_near, swapped_far)

    slab_steps = (STEPS, TX, AY, TZ)
    region = (PLANES, AY, TZ)
    f32 = jnp.float32
    padded = pltpu.VMEM((2, PLANES, AY + 2 * PAD, TZ), f32)
    matrix = pltpu.VMEM((2 * TZ, 2 * TZ), jnp.bfloat16)
    limit = pltpu.CompilerParams(vmem_limit_bytes=16 << 20)
    curvature, misfit, courant = pl.pallas_call(
        forward_kernel,
        in_specs=in_smem(4) + in_vmem(13),
        out_specs=in_vmem(3),
        out_shape=[
            jax.ShapeDtypeStruct(slab_steps, f32),
            jax.ShapeDtypeStruct((SLABS, STEPS, NREC), f32),
            jax.ShapeDtypeStruct(region, f32),
        ],
        scratch_shapes=[
            padded,
            pltpu.VMEM(region, f32),
            pltpu.VMEM((STEPS, TX * AY, TZ), f32),
            pltpu.VMEM(region, f32),
            matrix,
        ],
        compiler_params=limit,
        name="forward",
    )(
        aperture, source_cell, checkpoint, wavelet, observed, receivers, *fields,
        vel, vel_left, vel_right, vel_far_left, vel_far_right,
    )

    misfits = lax.all_to_all(misfit[:, None], DOM, 0, 0, tiled=True).reshape(SLABS, STEPS, NREC)

    terms = pl.pallas_call(
        adjoint_kernel,
        in_specs=in_smem(1) + in_vmem(11),
        out_specs=in_vmem(1)[0],
        out_shape=jax.ShapeDtypeStruct((4, TX + 1, 8, TZ), f32),
        scratch_shapes=[
            padded,
            pltpu.VMEM(region, f32),
            pltpu.VMEM((TX, AY, TZ), f32),
            pltpu.VMEM(region, f32),
            matrix,
            pltpu.VMEM((PLANES * AY, NREC), jnp.bfloat16),
        ],
        compiler_params=limit,
        name="adjoint",
    )(
        aperture, receivers, misfits, *fields,
        vel, courant, curvature,
    )
    landed = lax.all_to_all(terms, "yh", 0, 0, tiled=True)
    tags = jnp.arange(4, dtype=jnp.float32).reshape(4, 1, 1, 1, 1)
    sums = jnp.sum(jnp.where(landed[None, :, TX:] == tags, landed[None, :, 0:TX], 0.0), axis=1)
    landed = lax.all_to_all(sums, "x", 0, 0, tiled=True)
    return jnp.sum(landed, axis=0, keepdims=True)


def solution(mesh):
    split = Mesh(mesh.devices.reshape(4, 4, 2, 8, 2), SHOT + DOM)
    placed = (
        P(SHOT + DOM, None, None, None),
        P(SHOT, DOM, None),
        P(SHOT),
        P(SHOT, None),
        P(SHOT, None, None),
        P(SHOT, None),
        P(SHOT),
        P(SHOT, DOM, None, None),
        P(SHOT, DOM, None, None),
        P(SHOT, DOM, None, None),
        P(SHOT, DOM, None, None),
    )
    return jax.shard_map(
        inner,
        mesh=split,
        in_specs=placed,
        out_specs=P(SHOT + DOM, None, None, None),
        check_vma=False,
    )
```
